256 devices in a mesh: tgt: 16 (over y_hi, z), src: 8 (over x, y_lo), grp: 2 (over core).
Axes of the slice: x: 4, y: 4 (y_hi: 2, y_lo: 2; y = y_hi * 2 + y_lo), z: 8, core: 2. Of those that a mesh axis runs over, the one named last changes fastest.
Arguments:
- positions: float32 [3, 16384], P(None, ('tgt', 'src', 'grp')), may hold values from 0 to 1
- strengths: float32 [3, 16384], P(None, ('tgt', 'src', 'grp')), may hold values from -0.02 to 0.02
- live_counts: int32 [256], P(('tgt', 'src', 'grp')), may hold values from 1 to 64, 10240 in all
- vorticity: float32 [3, 192, 384, 256], P(None, 'tgt', ('src', 'grp')), may hold values from -6 to 6
- diffusivity: float32 [192, 384, 256], P('tgt', ('src', 'grp')), may hold values from 0.02 to 0.15
- seed_counts: int32 [192, 384, 256], P('tgt', ('src', 'grp')), may hold values from 0 to 7
Outputs:
- vorticity_next: float32 [3, 192, 384, 256], P(None, 'tgt', ('src', 'grp'))
- particle_rates: float32 [6, 16384], P(None, ('tgt', 'src', 'grp'))
- blob_velocity: float32 [3, 32768], P(None, ('tgt', 'src', 'grp'))
The draws below stay inside these ranges and needn't reach their ends.
Inputs may be any that keep to these rules, and one draw needn't show every extreme that they name: `live_counts`: the values sum to 256 * 64 * 5 // 8.
All inputs are finite; a program needn't handle non-finite values.
Results may differ from the reference program's by a relative error of at most 0.000095.
Values sent between devices are 32-bit elements; how exact they have to be, the bound alone decides.
A program may use at most 64 MiB of HBM per device.

```python
import math
import jax
import jax.numpy as jnp
import numpy as np
from jax import lax

P_DEV = 64
CX = 12
CY = 24
GZ = 256
BZ = 2
B_DEV = 128
E_DEV = 192
NP = 16384
GX = 192
GY = 384
N_TGT = 16
DEVICES = 256


def with_ends(entries, key, low, top_value):
    longest = entries.shape.index(max(entries.shape))
    spots = []
    for shift in (0, 1):
        where = [jax.random.randint(jax.random.fold_in(key, axis), (), 0, length) for axis, length in enumerate(entries.shape)]
        where[longest] = (where[longest] + shift) % entries.shape[longest]
        spots.append(tuple(where))
    return entries.at[spots[0]].set(low).at[spots[1]].set(top_value)


def level_of(own_key, shape, pieces, smallest, high):
    level, own = 1.0, jax.random.fold_in(own_key, 6)
    for position, shards_of in pieces:
        draws = jnp.exp(jax.random.uniform(jax.random.fold_in(own, position), (shards_of,), jnp.float32, smallest / len(pieces), high / len(pieces)))
        level = level * jnp.repeat(draws, shape[position] // shards_of).reshape([-1 if axis == position else 1 for axis in range(len(shape))])
    return level


def split_up(amount, total, limit, lean):
    weights = [(1 << 20) // math.isqrt(rank ** lean) + 1 for rank in range(2, amount + 1)]
    rest, holding = total - limit - (amount - 1), [1] * (amount - 1)
    while rest > 0:
        candidates = [i for i in range(amount - 1) if holding[i] < limit]
        pool, left = sum([weights[i] for i in candidates]), rest
        for i in candidates:
            addition = min(limit - holding[i], max(1, left * weights[i] // pool), rest)
            holding[i] = holding[i] + addition
            rest = rest - addition
    return np.array([limit] + holding)


def ragged_sizes(rng, number_of, total, reach, lean):
    if number_of == 2:
        one = jax.random.randint(rng, (), max(1, total - reach), min(reach, total - 1) + 1)
        return jnp.stack([one, total - one])
    lengths = jnp.asarray(split_up(number_of, total, reach, lean), jnp.int32)
    couples = (number_of - 1) // 2
    giver, sink = lengths[1:1 + 2 * couples:2], lengths[2:2 + 2 * couples:2]
    room = jnp.minimum(giver - 1, reach - sink)
    shifted = jax.random.randint(jax.random.fold_in(rng, 1), (couples,), 0, 1 << 20) % (room + 1)
    lengths = lengths.at[1:1 + 2 * couples:2].set(giver - shifted).at[2:2 + 2 * couples:2].set(sink + shifted)
    return lengths[jax.random.permutation(jax.random.fold_in(rng, 2), number_of)]


def gaussian(key, shape, width, most, shards=(), held_as=jnp.bfloat16):
    drawn = jax.random.normal(key, shape, jnp.float32) * width
    if len(shards) > 0:
        drawn = level_of(key, shape, shards, -0.22, 0.18) * drawn
    return jnp.clip(drawn, min=-most, max=most).astype(held_as)


def setup_inputs(seed: int = 0) -> dict:
    key_of = jax.random.split(jax.random.key(seed), 7)
    return {
        "positions": jnp.clip(1.0 * jax.random.uniform(key_of[0], (3, NP), jnp.float32) ** level_of(key_of[0], (3, NP), ((1, 256),), -0.2, 0.2), 0.0, 1.0),
        "strengths": gaussian(key_of[1], (3, NP), 0.003, 0.02, ((1, 256),), jnp.float32),
        "live_counts": ragged_sizes(key_of[2], DEVICES, DEVICES * P_DEV * 5 // 8, P_DEV, 2).astype(jnp.int32),
        "vorticity": gaussian(key_of[3], (3, GX, GY, GZ), 1.0, 6.0, ((1, 16), (2, 16)), jnp.float32),
        "diffusivity": jnp.clip(0.02 + 0.13000001 * jax.random.uniform(key_of[4], (GX, GY, GZ), jnp.float32) ** level_of(key_of[4], (GX, GY, GZ), ((0, 16), (1, 16)), -0.2, 0.2), 0.02, 0.15),
        "seed_counts": with_ends(jax.random.randint(key_of[5], (GX, GY, GZ), 0, 8), jax.random.fold_in(key_of[5], 1), 0, 7).astype(jnp.int32),
    }


sigma_sq = 0.0004
kernel_scale = 0.25 / 3.141592653589793
seed_weight = 0.0001

def pair_rates(targets, sources):
    sep_x = targets[0][:, None] - sources[0][None, :]
    sep_y = targets[1][:, None] - sources[1][None, :]
    sep_z = targets[2][:, None] - sources[2][None, :]
    squared = sep_x * sep_x + sep_y * sep_y + sep_z * sep_z + sigma_sq
    inverse = lax.rsqrt(squared)
    kernel = inverse * inverse * inverse
    kernel_five = kernel * inverse * inverse
    cross_x = sep_y * sources[5][None, :] - sep_z * sources[4][None, :]
    cross_y = sep_z * sources[3][None, :] - sep_x * sources[5][None, :]
    cross_z = sep_x * sources[4][None, :] - sep_y * sources[3][None, :]
    projected = targets[3][:, None] * sep_x + targets[4][:, None] * sep_y + targets[5][:, None] * sep_z
    weighted = 3.0 * kernel_five * projected
    velocity = jnp.stack([lax.optimization_barrier(jnp.sum(kernel * cross_x, axis=1)), lax.optimization_barrier(jnp.sum(kernel * cross_y, axis=1)), lax.optimization_barrier(jnp.sum(kernel * cross_z, axis=1))])
    pulled_x = lax.optimization_barrier(jnp.sum(kernel * sources[3][None, :], axis=1))
    pulled_y = lax.optimization_barrier(jnp.sum(kernel * sources[4][None, :], axis=1))
    pulled_z = lax.optimization_barrier(jnp.sum(kernel * sources[5][None, :], axis=1))
    first_term = jnp.stack([targets[4] * pulled_z - targets[5] * pulled_y, targets[5] * pulled_x - targets[3] * pulled_z, targets[3] * pulled_y - targets[4] * pulled_x])
    second_term = jnp.stack([lax.optimization_barrier(jnp.sum(weighted * cross_x, axis=1)), lax.optimization_barrier(jnp.sum(weighted * cross_y, axis=1)), lax.optimization_barrier(jnp.sum(weighted * cross_z, axis=1))])
    return (-kernel_scale * velocity, -kernel_scale * (first_term - second_term))

def laplace(padded):
    centre = padded[:, 1:-1, 1:-1, 1:-1]
    beside_all = padded[:, 2:, 1:-1, 1:-1] + padded[:, :-2, 1:-1, 1:-1]
    beside_all = beside_all + padded[:, 1:-1, 2:, 1:-1] + padded[:, 1:-1, :-2, 1:-1]
    beside_all = beside_all + padded[:, 1:-1, 1:-1, 2:] + padded[:, 1:-1, 1:-1, :-2]
    return beside_all - 6.0 * centre

def reference(positions, strengths, live_counts, vorticity, diffusivity, seed_counts):
    padded = jnp.pad(vorticity, ((0, 0), (1, 1), (1, 1), (1, 1)))
    vorticity_next = vorticity + diffusivity[None] * laplace(padded)
    counts = seed_counts.astype(jnp.float32)
    grid_y = vorticity.shape[2]
    y_slabs = grid_y // CY
    z_blocks = GZ // BZ
    blob_strength = seed_weight * lax.optimization_barrier(jnp.sum((vorticity_next * counts[None]).reshape(3, N_TGT, CX, y_slabs, CY, z_blocks, BZ), axis=(2, 4, 6)))
    blob_strength = blob_strength.reshape(3, DEVICES, B_DEV)
    weights = (counts + 1.0).reshape(N_TGT, CX, y_slabs, CY, z_blocks, BZ)
    totals = lax.optimization_barrier(jnp.sum(weights, axis=(1, 3, 5)))
    x_centres = ((jnp.arange(N_TGT * CX, dtype=jnp.float32) + 0.5) / GZ).reshape(N_TGT, CX)
    y_centres = ((jnp.arange(grid_y, dtype=jnp.float32) + 0.5) / GZ).reshape(y_slabs, CY)
    z_centres = ((jnp.arange(GZ, dtype=jnp.float32) + 0.5) / GZ).reshape(z_blocks, BZ)
    blob_x = lax.optimization_barrier(jnp.sum(lax.optimization_barrier(jnp.sum(weights, axis=(3, 5))) * x_centres[:, :, None, None], axis=1))
    blob_y = lax.optimization_barrier(jnp.sum(lax.optimization_barrier(jnp.sum(weights, axis=(1, 5))) * y_centres[None, :, :, None], axis=2))
    blob_z = lax.optimization_barrier(jnp.sum(lax.optimization_barrier(jnp.sum(weights, axis=(1, 3))) * z_centres[None, None], axis=3))
    blob_position = (jnp.stack([blob_x, blob_y, blob_z]) / totals[None]).reshape(3, DEVICES, B_DEV)
    live_mask = (jnp.arange(P_DEV, dtype=jnp.int32)[None, :] < live_counts[:, None]).astype(jnp.float32)
    particle_pos = positions.reshape(3, DEVICES, P_DEV)
    particle_str = strengths.reshape(3, DEVICES, P_DEV) * live_mask[None]
    elements = jnp.concatenate([jnp.concatenate([particle_pos, blob_position], axis=2), jnp.concatenate([particle_str, blob_strength], axis=2)], axis=0)
    sources = elements.reshape(6, DEVICES * E_DEV)

    def per_device(targets):
        velocity, stretch = pair_rates(targets, sources)
        return jnp.concatenate([velocity, stretch], axis=0)
    all_rates = lax.map(per_device, jnp.moveaxis(elements, 1, 0))
    particle_rates = jnp.moveaxis(all_rates[:, :, :P_DEV] * live_mask[:, None, :], 0, 1).reshape(6, DEVICES * P_DEV)
    blob_velocity = jnp.moveaxis(all_rates[:, :3, P_DEV:], 0, 1).reshape(3, DEVICES * B_DEV)
    return (vorticity_next, particle_rates, blob_velocity)
```

```python
import jax
import jax.numpy as jnp
from jax import lax
from jax.experimental import pallas as pl
from jax.experimental.pallas import tpu as pltpu
from jax.sharding import PartitionSpec as P

kernel_scale = 0.25 / 3.141592653589793
seed_weight = 0.0001

SIGMA = 0.0004
F32, BF16 = jnp.float32, jnp.bfloat16
PAIRS = ((0, 8), (1, 2), (3, 4), (5, 6), (7, 9), (10, 11), (12, 13), (14, 15))
NS = 9


def cross(a, b):
    return (
        a[1] * b[2] - a[2] * b[1],
        a[2] * b[0] - a[0] * b[2],
        a[0] * b[1] - a[1] * b[0],
    )


def pieces(rows):
    one = rows.astype(BF16)
    rest = rows - one.astype(F32)
    two = rest.astype(BF16)
    three = (rest - two.astype(F32)).astype(BF16)
    return one, two, three


def weights_of(rows):
    x = [rows[c : c + 1] for c in range(3)]
    a = [rows[c + 3 : c + 4] for c in range(3)]
    b = cross(x, a)
    zero = jnp.zeros_like(a[0])
    return jnp.concatenate([*a, *b, zero, zero], axis=0)


def stacked(rows):
    one, two, three = pieces(rows)
    return jnp.concatenate([one, two, three, jnp.zeros_like(one)], axis=0)


def fold3(m):
    return m[0:8] + m[8:16] + m[16:24]


def fold2(m):
    return m[0:8] + m[8:16]


NN = (((1,), (0,)), ((), ()))
NT = (((1,), (1,)), ((), ()))


def mm(a, b, dims):
    return lax.dot_general(a, b, dims, preferred_element_type=F32)


def pair_kernel(tb, tp, sb, sp, rt, rs, tr, wt, wtm, ws, scol, acol, acct, acct5, accs, accs5, khi, klo, qhi, qlo, uhi, ulo):
    lane = lax.broadcasted_iota(jnp.int32, (8, 128), 1)
    lane2 = lax.broadcasted_iota(jnp.int32, (1, 256), 1)
    for blk in range(12):
        halves = []
        for h in range(2):
            if blk < 8:
                halves.append(tb[2 * blk + h])
            else:
                one, two = PAIRS[2 * (blk - 8) + h]
                halves.append(jnp.where(lane < 64, tp[one], pltpu.roll(tp[two], 64, 1)))
        rows = jnp.concatenate(halves, axis=1)
        tr[blk] = rows
        w = weights_of(rows)
        wt[blk] = stacked(w)
        if blk < 5:
            keep = {0: (0, 1), 4: (0, 0)}.get(blk, (1, 1))
            keep = [keep[0], keep[0], keep[1], keep[1]]
        elif 8 <= blk < 11:
            slots = [s for h in range(2) for s in PAIRS[2 * (blk - 8) + h]]
            keep = [int(1 <= s <= 7) for s in slots]
        else:
            continue
        mask = jnp.zeros((1, 256), F32)
        for quarter in range(4):
            if keep[quarter]:
                mask = jnp.where((lane2 >= 64 * quarter) & (lane2 < 64 * quarter + 64), 1.0, mask)
        wtm[blk] = stacked(w * mask)
    for slot in range(NS):
        rows = jnp.concatenate([sb[slot], sp[slot]], axis=1)
        ws[slot] = stacked(weights_of(rows))
        blob = sb[slot].T
        part = sp[slot].T
        for c in range(3):
            scol[c, slot, 0:128, :] = jnp.broadcast_to(blob[:, c : c + 1], (128, 128))
            scol[c, slot, 128:192, :] = jnp.broadcast_to(part[:64, c : c + 1], (64, 128))
            acol[c, slot, :, :] = jnp.broadcast_to(part[:64, c + 3 : c + 4] * -3.0, (64, 128))
    acct[...] = jnp.zeros_like(acct)
    acct5[...] = jnp.zeros_like(acct5)
    accs[...] = jnp.zeros_like(accs)
    accs5[...] = jnp.zeros_like(accs5)

    def block(slot, blk, part, wref, tmask):
        for h in range(2):
            t = [tr[blk, c : c + 1, 128 * h : 128 * h + 128] for c in range(6)]
            tx = [jnp.broadcast_to(v, (16, 128)) for v in t[:3]]
            if part:
                ta = [jnp.broadcast_to(v * 3.0, (16, 128)) for v in t[3:]]
            for g in range(12):
                rows = slice(16 * g, 16 * g + 16)
                cols = slice(128 * h, 128 * h + 128)
                d = [tx[c] - scol[c, slot, rows, :] for c in range(3)]
                q = (d[0] * d[0] + d[1] * d[1]) + (d[2] * d[2] + SIGMA)
                inv = lax.rsqrt(q)
                inv2 = inv * inv
                k = inv2 * inv
                hi = k.astype(BF16)
                khi[rows, cols] = hi
                klo[rows, cols] = (k - hi.astype(F32)).astype(BF16)
                if part or g >= 8:
                    k5 = k * inv2
                if part:
                    p = (ta[0] * d[0] + ta[1] * d[1]) + ta[2] * d[2]
                    s = k5 * p
                    hi = s.astype(BF16)
                    qhi[rows, cols] = hi
                    qlo[rows, cols] = (s - hi.astype(F32)).astype(BF16)
                if g >= 8:
                    part_rows = slice(16 * (g - 8), 16 * (g - 8) + 16)
                    p = (acol[0, slot, part_rows, :] * d[0] + acol[1, slot, part_rows, :] * d[1]) + acol[2, slot, part_rows, :] * d[2]
                    s = k5 * p
                    hi = s.astype(BF16)
                    uhi[part_rows, cols] = hi
                    ulo[part_rows, cols] = (s - hi.astype(F32)).astype(BF16)
        w = ws[slot][:, :192]
        to_t = fold3(mm(w, khi[...], NN)) + fold2(mm(w[:16], klo[...], NN))
        if tmask is not None:
            to_t = to_t * tmask
        acct[blk] += to_t
        if part:
            to_t5 = fold3(mm(w, qhi[...], NN)) + fold2(mm(w[:16], qlo[...], NN))
            if tmask is not None:
                to_t5 = to_t5 * tmask
            acct5[blk - 8] += to_t5
        if wref is not None:
            v = wref[blk]
            accs[slot, :, :192] += fold3(mm(v, khi[...], NT)) + fold2(mm(v[:16], klo[...], NT))
            accs5[slot, :, :64] += fold3(mm(v, uhi[...], NT)) + fold2(mm(v[:16], ulo[...], NT))

    @pl.loop(1, 8)
    def _(slot):
        @pl.loop(0, 8)
        def _(blk):
            block(slot, blk, False, wt, None)

        @pl.loop(8, 12)
        def _(blk):
            block(slot, blk, True, wt, None)

    @pl.loop(0, 2)
    def _(which):
        slot = which * 8

        @pl.loop(0, 5)
        def _(blk):
            block(slot, blk, False, wtm, jnp.where((lane2 < 128) | (blk < 4), 1.0, 0.0))

        @pl.loop(8, 11)
        def _(blk):
            block(slot, blk, True, wtm, jnp.where((lane2 < 64) | (blk < 10), 1.0, 0.0))

    def finish(rows, acc, acc5):
        x = [rows[c : c + 1] for c in range(3)]
        a = [rows[c + 3 : c + 4] for c in range(3)]
        sums = [acc[c : c + 1] for c in range(6)]
        vel = [m - n for m, n in zip(cross(x, sums[:3]), sums[3:])]
        if acc5 is None:
            return vel
        sums5 = [acc5[c : c + 1] for c in range(6)]
        turn = cross(a, sums[:3])
        pull = cross(x, sums5[:3])
        return vel + [turn[c] - (pull[c] - sums5[3 + c]) for c in range(3)]

    pad2 = jnp.zeros((2, 256), F32)
    pad5 = jnp.zeros((5, 256), F32)
    for blk in range(12):
        rows = tr[blk]
        if blk < 8:
            out = jnp.concatenate([*finish(rows, acct[blk], None), pad5], axis=0)
            rt[2 * blk, :, 0:128] = out[:, :128]
            rt[2 * blk + 1, :, 0:128] = out[:, 128:]
        else:
            out = jnp.concatenate([*finish(rows, acct[blk], acct5[blk - 8]), pad2], axis=0)
            for h in range(2):
                one, two = PAIRS[2 * (blk - 8) + h]
                half = out[:, 128 * h : 128 * h + 128]
                rt[one, :, 128:256] = half
                rt[two, :, 128:256] = pltpu.roll(half, 64, 1)
    for slot in range(NS):
        rows = jnp.concatenate([sb[slot], sp[slot]], axis=1)
        acc = accs[slot]
        vel = finish(rows, acc, None)
        five = accs5[slot]
        full = finish(rows[:, 128:], acc[:, 128:], five)
        rs[slot, :, 0:128] = jnp.concatenate([v[:, :128] for v in vel] + [pad5[:, :128]], axis=0)
        rs[slot, :, 128:256] = jnp.concatenate([*full, pad2[:, :128]], axis=0)


def pair_call(tb, tp, sb, sp):
    return pl.pallas_call(
        pair_kernel,
        out_shape=(jax.ShapeDtypeStruct((16, 8, 256), F32), jax.ShapeDtypeStruct((NS, 8, 256), F32)),
        in_specs=[pl.BlockSpec(memory_space=pltpu.VMEM)] * 4,
        out_specs=(pl.BlockSpec(memory_space=pltpu.VMEM),) * 2,
        scratch_shapes=[
            pltpu.VMEM((12, 8, 256), F32),
            pltpu.VMEM((12, 32, 256), BF16),
            pltpu.VMEM((12, 32, 256), BF16),
            pltpu.VMEM((NS, 32, 256), BF16),
            pltpu.VMEM((3, NS, 192, 128), F32),
            pltpu.VMEM((3, NS, 64, 128), F32),
            pltpu.VMEM((12, 8, 256), F32),
            pltpu.VMEM((4, 8, 256), F32),
            pltpu.VMEM((NS, 8, 256), F32),
            pltpu.VMEM((NS, 8, 128), F32),
            pltpu.VMEM((192, 256), BF16),
            pltpu.VMEM((192, 256), BF16),
            pltpu.VMEM((192, 256), BF16),
            pltpu.VMEM((192, 256), BF16),
            pltpu.VMEM((64, 256), BF16),
            pltpu.VMEM((64, 256), BF16),
        ],
        compiler_params=pltpu.CompilerParams(vmem_limit_bytes=48 * 1024 * 1024),
        name="pairs",
    )(tb, tp, sb, sp)


MESH = pl.DeviceIdType.MESH
RING = 16


def place():
    return lax.axis_index("tgt"), lax.axis_index("src") * 2 + lax.axis_index("grp")


def on_tgt(u):
    return {"tgt": lax.rem(u, RING)}


def on_side(p):
    p = lax.rem(p, RING)
    return {"src": p // 2, "grp": lax.rem(p, 2)}


def grid_kernel(vort, diff, seeds, pos, stren, live, vnext, otb, otp, osb, osp, hx, hy, sy, elp, elb, gtb, gtp, gsb, gsp, accs, accw, halo_send, halo_recv, tps, tpr, sps, spr, tbs, tbr, sbs, sbr):
    u, p = place()
    barrier = pltpu.get_barrier_semaphore()

    @pl.loop(1, RING)
    def _(d):
        pl.semaphore_signal(barrier, inc=1, device_id=on_tgt(u + d), device_id_type=MESH)
        pl.semaphore_signal(barrier, inc=1, device_id=on_side(p + d), device_id_type=MESH)

    nx, ny, nz = diff.shape
    for c in range(3):
        sy[0, 16 * c : 16 * c + nx, :] = vort[c, :, 0, :]
        sy[1, 16 * c : 16 * c + nx, :] = vort[c, :, ny - 1, :]
    slots = pos.shape[1]
    elp[...] = jnp.zeros_like(elp)
    elp[0:3, 0:slots] = pos[...]
    lane = lax.broadcasted_iota(jnp.int32, (3, slots), 1)
    elp[3:6, 0:slots] = jnp.where(lane < live[0], stren[...], 0.0)
    pl.semaphore_wait(barrier, 2 * (RING - 1))

    halos = []
    for n, (src, dst, to) in enumerate(
        (
            (vort.at[:, 0], hx.at[1], on_tgt(u + RING - 1)),
            (vort.at[:, nx - 1], hx.at[0], on_tgt(u + 1)),
            (sy.at[0], hy.at[1], on_side(p + RING - 1)),
            (sy.at[1], hy.at[0], on_side(p + 1)),
        )
    ):
        halos.append(pltpu.make_async_remote_copy(src, dst, halo_send.at[n], halo_recv.at[n], device_id=to, device_id_type=MESH))
    for copy in halos:
        copy.start()

    def tgt_copy(src, held, send, recv, d):
        return pltpu.make_async_remote_copy(src, held.at[RING - d], send.at[d - 1], recv.at[RING - 1 - d], device_id=on_tgt(u + d), device_id_type=MESH)

    def side_copy(src, held, send, recv, d):
        return pltpu.make_async_remote_copy(src, held.at[d], send.at[d - 1], recv.at[d - 1], device_id=on_side(p + RING - d), device_id_type=MESH)

    @pl.loop(1, RING)
    def _(d):
        tgt_copy(elp, gtp, tps, tpr, d).start()

    @pl.loop(1, NS)
    def _(d):
        side_copy(elp, gsp, sps, spr, d).start()

    row = lax.broadcasted_iota(jnp.int32, (ny, nz), 0)
    col = lax.broadcasted_iota(jnp.int32, (ny, nz), 1)
    accs[...] = jnp.zeros_like(accs)
    accw[...] = jnp.zeros_like(accw)

    def plane(i, low, high):
        counts = seeds[i].astype(F32)
        weight = counts + 1.0
        accw[0] += weight
        accw[1] += weight * jnp.asarray(i, jnp.int32).astype(F32)
        rate = diff[i]
        for c in range(3):
            v = vort[c, i]
            beside = jnp.where(row > 0, pltpu.roll(v, 1, 0), 0.0)
            beside += jnp.where(row < ny - 1, pltpu.roll(v, ny - 1, 0), 0.0)
            beside += jnp.where(col > 0, pltpu.roll(v, 1, 1), 0.0)
            beside += jnp.where(col < nz - 1, pltpu.roll(v, nz - 1, 1), 0.0)
            if low:
                beside += vort[c, i - 1]
            if high:
                beside += vort[c, i + 1]
            new = v + rate * (beside - 6.0 * v)
            vnext[c, i] = new
            accs[c] += counts * new

    plane(0, False, True)

    @pl.loop(1, nx - 1)
    def _(i):
        plane(i, True, True)

    plane(nx - 1, True, False)

    for copy in halos:
        copy.wait()
    sides = [
        [(u > 0).astype(F32), (u < RING - 1).astype(F32)],
        [(p > 0).astype(F32), (p < RING - 1).astype(F32)],
    ]
    extra = []
    for end, i in enumerate((0, nx - 1)):
        counts = seeds[i].astype(F32)
        rate = diff[i] * sides[0][end]
        for c in range(3):
            more = rate * hx[end, c]
            vnext[c, i] += more
            accs[c] += counts * more
    edge = [jnp.zeros((1, nz), F32) for _ in range(3)]
    for end, j in enumerate((0, ny - 1)):
        counts = seeds[:, j, :].astype(F32)
        rate = diff[:, j, :] * sides[1][end]
        for c in range(3):
            more = rate * hy[end, 16 * c : 16 * c + nx, :]
            vnext[c, :, j, :] = vnext[c, :, j, :] + more
            edge[c] = edge[c] + jnp.sum(counts * more, axis=0, keepdims=True)

    weight = accw[0]
    odd = jnp.where(lax.rem(col, 2) == 1, weight, 0.0)
    sums = [jnp.sum(accs[c], axis=0, keepdims=True) + edge[c] for c in range(3)]
    sums += [jnp.sum(m, axis=0, keepdims=True) for m in (weight, accw[1], weight * row.astype(F32), odd)]
    sums.append(jnp.zeros((1, nz), F32))
    half = (lax.broadcasted_iota(jnp.int32, (nz, nz // 2), 0) // 2 == lax.broadcasted_iota(jnp.int32, (nz, nz // 2), 1)).astype(F32)
    folded = jnp.dot(jnp.concatenate(sums, axis=0), half, precision=lax.Precision.HIGHEST, preferred_element_type=F32)
    total = folded[3:4]
    block = lax.broadcasted_iota(jnp.int32, (1, nz // 2), 1).astype(F32)
    x = ((u * nx).astype(F32) + 0.5 + folded[4:5] / total) / nz
    y = ((p * ny).astype(F32) + 0.5 + folded[5:6] / total) / nz
    z = (2.0 * block + 0.5 + folded[6:7] / total) / nz
    zero = jnp.zeros_like(x)
    elb[...] = jnp.concatenate([x, y, z, *[folded[c : c + 1] * seed_weight for c in range(3)], zero, zero], axis=0)

    @pl.loop(1, RING)
    def _(d):
        tgt_copy(elb, gtb, tbs, tbr, d).start()

    @pl.loop(1, NS)
    def _(d):
        side_copy(elb, gsb, sbs, sbr, d).start()

    gtb[0] = elb[...]
    gsb[0] = elb[...]
    gtp[0] = elp[...]
    gsp[0] = elp[...]

    @pl.loop(1, RING)
    def _(d):
        tgt_copy(elp, gtp, tps, tpr, d).wait()
        tgt_copy(elb, gtb, tbs, tbr, d).wait()

    @pl.loop(1, NS)
    def _(d):
        side_copy(elp, gsp, sps, spr, d).wait()
        side_copy(elb, gsb, sbs, sbr, d).wait()

    otb[...] = gtb[...]
    otp[...] = gtp[...]
    osb[...] = gsb[...]
    osp[...] = gsp[...]


def grid_call(positions, strengths, live_counts, vorticity, diffusivity, seed_counts):
    nx, ny, nz = diffusivity.shape
    vmem = pl.BlockSpec(memory_space=pltpu.VMEM)
    dma = pltpu.SemaphoreType.DMA
    return pl.pallas_call(
        grid_kernel,
        out_shape=(
            jax.ShapeDtypeStruct(vorticity.shape, F32),
            jax.ShapeDtypeStruct((16, 8, 128), F32),
            jax.ShapeDtypeStruct((16, 8, 128), F32),
            jax.ShapeDtypeStruct((NS, 8, 128), F32),
            jax.ShapeDtypeStruct((NS, 8, 128), F32),
        ),
        in_specs=[vmem] * 5 + [pl.BlockSpec(memory_space=pltpu.SMEM)],
        out_specs=(vmem,) * 5,
        scratch_shapes=[
            pltpu.VMEM((2, 3, ny, nz), F32),
            pltpu.VMEM((2, 48, nz), F32),
            pltpu.VMEM((2, 48, nz), F32),
            pltpu.VMEM((8, 128), F32),
            pltpu.VMEM((8, 128), F32),
            pltpu.VMEM((16, 8, 128), F32),
            pltpu.VMEM((16, 8, 128), F32),
            pltpu.VMEM((NS, 8, 128), F32),
            pltpu.VMEM((NS, 8, 128), F32),
            pltpu.VMEM((3, ny, nz), F32),
            pltpu.VMEM((2, ny, nz), F32),
            dma((4,)),
            dma((4,)),
            dma((15,)),
            dma((15,)),
            dma((8,)),
            dma((8,)),
            dma((15,)),
            dma((15,)),
            dma((8,)),
            dma((8,)),
        ],
        compiler_params=pltpu.CompilerParams(vmem_limit_bytes=32 * 1024 * 1024, collective_id=0, has_side_effects=True),
        name="grid",
    )(vorticity, diffusivity, seed_counts, positions, strengths, live_counts)


def sum_kernel(rt, rs, live, rates, blob, it, is_, tsend, trecv, ssend, srecv):
    u, p = place()
    barrier = pltpu.get_barrier_semaphore()

    @pl.loop(1, RING)
    def _(d):
        pl.semaphore_signal(barrier, inc=1, device_id=on_tgt(u + d), device_id_type=MESH)

        pl.semaphore_signal(barrier, inc=1, device_id=on_side(p + d), device_id_type=MESH)

    pl.semaphore_wait(barrier, 2 * (RING - 1))

    def tgt_copy(d):
        return pltpu.make_async_remote_copy(rt.at[d], it.at[d - 1], tsend.at[d - 1], trecv.at[d - 1], device_id=on_tgt(u + d), device_id_type=MESH)

    def side_copy(d):
        return pltpu.make_async_remote_copy(rs.at[d], is_.at[d - 1], ssend.at[d - 1], srecv.at[d - 1], device_id=on_side(p + d), device_id_type=MESH)

    @pl.loop(1, RING)
    def _(d):
        tgt_copy(d).start()

    @pl.loop(1, NS)
    def _(d):
        side_copy(d).start()

    @pl.loop(1, RING)
    def _(d):
        tgt_copy(d).wait()

    @pl.loop(1, NS)
    def _(d):
        side_copy(d).wait()

    total = rt[0] + rs[0]
    for n in range(RING - 1):
        total = total + it[n]
    for n in range(NS - 1):
        total = total + is_[n]
    total = total * -kernel_scale
    slots = rates.shape[1]
    lane = lax.broadcasted_iota(jnp.int32, (6, slots), 1)
    rates[...] = jnp.where(lane < live[0], total[0:6, 128 : 128 + slots], 0.0)
    blob[...] = total[0:3, 0:128]


def sum_call(rt, rs, live_counts):
    vmem = pl.BlockSpec(memory_space=pltpu.VMEM)
    dma = pltpu.SemaphoreType.DMA
    return pl.pallas_call(
        sum_kernel,
        out_shape=(jax.ShapeDtypeStruct((6, 64), F32), jax.ShapeDtypeStruct((3, 128), F32)),
        in_specs=[vmem, vmem, pl.BlockSpec(memory_space=pltpu.SMEM)],
        out_specs=(vmem, vmem),
        scratch_shapes=[
            pltpu.VMEM((15, 8, 256), F32),
            pltpu.VMEM((NS - 1, 8, 256), F32),
            dma((15,)),
            dma((15,)),
            dma((NS - 1,)),
            dma((NS - 1,)),
        ],
        compiler_params=pltpu.CompilerParams(vmem_limit_bytes=16 * 1024 * 1024, collective_id=1, has_side_effects=True),
        name="sums",
    )(rt, rs, live_counts)


def per_device(positions, strengths, live_counts, vorticity, diffusivity, seed_counts):
    vorticity_next, tb, tp, sb, sp = grid_call(positions, strengths, live_counts, vorticity, diffusivity, seed_counts)
    rt, rs = pair_call(tb, tp, sb, sp)
    particle_rates, blob_velocity = sum_call(rt, rs, live_counts)
    return vorticity_next, particle_rates, blob_velocity


def solution(mesh):
    placed = (
        P(None, ("tgt", "src", "grp")),
        P(None, ("tgt", "src", "grp")),
        P(("tgt", "src", "grp")),
        P(None, "tgt", ("src", "grp"), None),
        P("tgt", ("src", "grp"), None),
        P("tgt", ("src", "grp"), None),
    )
    return jax.shard_map(
        per_device,
        mesh=mesh,
        in_specs=placed,
        out_specs=(
            P(None, "tgt", ("src", "grp"), None),
            P(None, ("tgt", "src", "grp")),
            P(None, ("tgt", "src", "grp")),
        ),
        check_vma=False,
    )
```

```python
import jax
import jax.numpy as jnp
from jax import lax
from jax.experimental import pallas as pl
from jax.experimental.pallas import tpu as pltpu
from jax.sharding import PartitionSpec as P

kernel_scale = 0.25 / 3.141592653589793
seed_weight = 0.0001

SIGMA = 0.0004
F32, BF16 = jnp.float32, jnp.bfloat16
PAIRS = ((0, 8), (1, 2), (3, 4), (5, 6), (7, 9), (10, 11), (12, 13), (14, 15))
NS = 9


def cross(a, b):
    return (
        a[1] * b[2] - a[2] * b[1],
        a[2] * b[0] - a[0] * b[2],
        a[0] * b[1] - a[1] * b[0],
    )


def pieces(rows):
    one = rows.astype(BF16)
    rest = rows - one.astype(F32)
    two = rest.astype(BF16)
    three = (rest - two.astype(F32)).astype(BF16)
    return one, two, three


def weights_of(rows):
    x = [rows[c : c + 1] for c in range(3)]
    a = [rows[c + 3 : c + 4] for c in range(3)]
    b = cross(x, a)
    zero = jnp.zeros_like(a[0])
    return jnp.concatenate([*a, *b, zero, zero], axis=0)


def stacked(rows):
    one, two, three = pieces(rows)
    return jnp.concatenate([one, two, three, jnp.zeros_like(one)], axis=0)


def fold3(m):
    return m[0:8] + m[8:16] + m[16:24]


def fold2(m):
    return m[0:8] + m[8:16]


NN = (((1,), (0,)), ((), ()))
NT = (((1,), (1,)), ((), ()))


def mm(a, b, dims):
    return lax.dot_general(a, b, dims, preferred_element_type=F32)


MESH = pl.DeviceIdType.MESH
RING = 16


def place():
    tgt, src = lax.axis_index("tgt"), lax.axis_index("src")
    return src * 2 + tgt // 8, lax.rem(tgt, 8) * 2 + lax.axis_index("grp")


def on_plane(a):
    a = lax.rem(a, RING)
    return {"tgt": lax.rem(a, 2) * 8 + lax.rem(lax.axis_index("tgt"), 8), "src": a // 2}


def on_line(b):
    b = lax.rem(b, RING)
    return {"tgt": (lax.axis_index("tgt") // 8) * 8 + b // 2, "grp": lax.rem(b, 2)}


def on_tgt(u):
    return {"tgt": lax.rem(u, RING)}


def on_side(p):
    p = lax.rem(p, RING)
    return {"src": p // 2, "grp": lax.rem(p, 2)}


def step_kernel(vort_in, diff_in, seeds_in, pos_in, stren_in, live, vnext, rates, blob, vort, diff, seeds, pos, stren, local, hx, hy, sy, elp, elb, gtb, gtp, gsb, gsp, gaccs, accw, halo_send, halo_recv, tps, tpr, sps, spr, tbs, tbr, sbs, sbr, vnew, out_sem, rt, rs, tr, wt, ws, scol, acol, acct, acct5, accs, accs5, tmask, khi0, klo0, qhi0, qlo0, uhi0, ulo0, khi1, klo1, qhi1, qlo1, uhi1, ulo1, it, is_, tsend, trecv, ssend, srecv):
    u, p = lax.axis_index("tgt"), lax.axis_index("src") * 2 + lax.axis_index("grp")
    a, b = place()
    fetch = [pltpu.make_async_copy(src, dst, local.at[n]) for n, (src, dst) in enumerate(((pos_in, pos), (stren_in, stren), (vort_in, vort), (diff_in, diff), (seeds_in, seeds)))]
    for copy in fetch:
        copy.start()
    barrier = pltpu.get_barrier_semaphore()
    for to in (on_tgt(u + 1), on_tgt(u + RING - 1), on_side(p + 1), on_side(p + RING - 1)):
        pl.semaphore_signal(barrier, inc=1, device_id=to, device_id_type=MESH)

    @pl.loop(1, RING)
    def _(d):
        pl.semaphore_signal(barrier, inc=1, device_id=on_plane(a + d), device_id_type=MESH)
        pl.semaphore_signal(barrier, inc=1, device_id=on_line(b + d), device_id_type=MESH)

    nx, ny, nz = diff.shape
    fetch[0].wait()
    fetch[1].wait()
    fetch[2].wait()
    for c in range(3):
        sy[0, 16 * c : 16 * c + nx, :] = vort[c, :, 0, :]
        sy[1, 16 * c : 16 * c + nx, :] = vort[c, :, ny - 1, :]
    slots = pos.shape[1]
    elp[...] = jnp.zeros_like(elp)
    elp[0:3, 0:slots] = pos[...]
    lane = lax.broadcasted_iota(jnp.int32, (3, slots), 1)
    elp[3:6, 0:slots] = jnp.where(lane < live[0], stren[...], 0.0)
    pl.semaphore_wait(barrier, 2 * (RING - 1) + 4)

    halos = []
    for n, (src, dst, to) in enumerate(
        (
            (vort.at[:, 0], hx.at[1], on_tgt(u + RING - 1)),
            (vort.at[:, nx - 1], hx.at[0], on_tgt(u + 1)),
            (sy.at[0], hy.at[1], on_side(p + RING - 1)),
            (sy.at[1], hy.at[0], on_side(p + 1)),
        )
    ):
        halos.append(pltpu.make_async_remote_copy(src, dst, halo_send.at[n], halo_recv.at[n], device_id=to, device_id_type=MESH))
    for copy in halos:
        copy.start()

    def tgt_copy(src, held, send, recv, d):
        return pltpu.make_async_remote_copy(src, held.at[RING - d], send.at[d - 1], recv.at[RING - 1 - d], device_id=on_plane(a + d), device_id_type=MESH)

    def side_copy(src, held, send, recv, d):
        return pltpu.make_async_remote_copy(src, held.at[d], send.at[d - 1], recv.at[d - 1], device_id=on_line(b + RING - d), device_id_type=MESH)

    @pl.loop(1, RING)
    def _(d):
        tgt_copy(elp, gtp, tps, tpr, d).start()

    @pl.loop(1, NS)
    def _(d):
        side_copy(elp, gsp, sps, spr, d).start()

    fetch[3].wait()
    fetch[4].wait()
    row = lax.broadcasted_iota(jnp.int32, (ny, nz), 0)
    col = lax.broadcasted_iota(jnp.int32, (ny, nz), 1)
    gaccs[...] = jnp.zeros_like(gaccs)
    accw[...] = jnp.zeros_like(accw)

    def plane(i, low, high):
        counts = seeds[i].astype(F32)
        weight = counts + 1.0
        accw[0] += weight
        accw[1] += weight * jnp.asarray(i, jnp.int32).astype(F32)
        rate = diff[i]
        for c in range(3):
            v = vort[c, i]
            beside = jnp.where(row > 0, pltpu.roll(v, 1, 0), 0.0)
            beside += jnp.where(row < ny - 1, pltpu.roll(v, ny - 1, 0), 0.0)
            beside += jnp.where(col > 0, pltpu.roll(v, 1, 1), 0.0)
            beside += jnp.where(col < nz - 1, pltpu.roll(v, nz - 1, 1), 0.0)
            if low:
                beside += vort[c, i - 1]
            if high:
                beside += vort[c, i + 1]
            new = v + rate * (beside - 6.0 * v)
            vnew[c, i] = new
            gaccs[c] += counts * new

    plane(0, False, True)

    @pl.loop(1, nx - 1)
    def _(i):
        plane(i, True, True)

    plane(nx - 1, True, False)

    for copy in halos:
        copy.wait()
    sides = [
        [(u > 0).astype(F32), (u < RING - 1).astype(F32)],
        [(p > 0).astype(F32), (p < RING - 1).astype(F32)],
    ]
    extra = []
    for end, i in enumerate((0, nx - 1)):
        counts = seeds[i].astype(F32)
        rate = diff[i] * sides[0][end]
        for c in range(3):
            more = rate * hx[end, c]
            vnew[c, i] += more
            gaccs[c] += counts * more
    edge = [jnp.zeros((1, nz), F32) for _ in range(3)]
    for end, j in enumerate((0, ny - 1)):
        counts = seeds[:, j, :].astype(F32)
        rate = diff[:, j, :] * sides[1][end]
        for c in range(3):
            more = rate * hy[end, 16 * c : 16 * c + nx, :]
            vnew[c, :, j, :] = vnew[c, :, j, :] + more
            edge[c] = edge[c] + jnp.sum(counts * more, axis=0, keepdims=True)

    leave = pltpu.make_async_copy(vnew, vnext, out_sem)
    leave.start()
    weight = accw[0]
    odd = jnp.where(lax.rem(col, 2) == 1, weight, 0.0)
    sums = [jnp.sum(gaccs[c], axis=0, keepdims=True) + edge[c] for c in range(3)]
    sums += [jnp.sum(m, axis=0, keepdims=True) for m in (weight, accw[1], weight * row.astype(F32), odd)]
    sums.append(jnp.zeros((1, nz), F32))
    half = (lax.broadcasted_iota(jnp.int32, (nz, nz // 2), 0) // 2 == lax.broadcasted_iota(jnp.int32, (nz, nz // 2), 1)).astype(F32)
    folded = jnp.dot(jnp.concatenate(sums, axis=0), half, precision=lax.Precision.HIGHEST, preferred_element_type=F32)
    total = folded[3:4]
    block = lax.broadcasted_iota(jnp.int32, (1, nz // 2), 1).astype(F32)
    x = ((u * nx).astype(F32) + 0.5 + folded[4:5] / total) / nz
    y = ((p * ny).astype(F32) + 0.5 + folded[5:6] / total) / nz
    z = (2.0 * block + 0.5 + folded[6:7] / total) / nz
    zero = jnp.zeros_like(x)
    elb[...] = jnp.concatenate([x, y, z, *[folded[c : c + 1] * seed_weight for c in range(3)], zero, zero], axis=0)

    @pl.loop(1, RING)
    def _(d):
        tgt_copy(elb, gtb, tbs, tbr, d).start()

    @pl.loop(1, NS)
    def _(d):
        side_copy(elb, gsb, sbs, sbr, d).start()

    gtb[0] = elb[...]
    gsb[0] = elb[...]
    gtp[0] = elp[...]
    gsp[0] = elp[...]

    @pl.loop(1, RING)
    def _(d):
        tgt_copy(elp, gtp, tps, tpr, d).wait()
        tgt_copy(elb, gtb, tbs, tbr, d).wait()

    @pl.loop(1, NS)
    def _(d):
        side_copy(elp, gsp, sps, spr, d).wait()
        side_copy(elb, gsb, sbs, sbr, d).wait()

    lane = lax.broadcasted_iota(jnp.int32, (8, 128), 1)
    lane2 = lax.broadcasted_iota(jnp.int32, (1, 256), 1)
    for blk in range(12):
        halves = []
        for h in range(2):
            if blk < 8:
                halves.append(gtb[2 * blk + h])
            else:
                one, two = PAIRS[2 * (blk - 8) + h]
                halves.append(jnp.where(lane < 64, gtp[one], pltpu.roll(gtp[two], 64, 1)))
        rows = jnp.concatenate(halves, axis=1)
        tr[blk] = rows
        w = weights_of(rows)
        wt[blk] = stacked(w)
        tmask[blk] = jnp.ones((1, 256), F32)
        slots = [2 * blk, 2 * blk, 2 * blk + 1, 2 * blk + 1] if blk < 8 else [s for h in range(2) for s in PAIRS[2 * (blk - 8) + h]]
        both = jnp.zeros((1, 256), F32)
        here = jnp.zeros((1, 256), F32)
        for n, slot in enumerate(slots):
            quarter = (lane2 >= 64 * n) & (lane2 < 64 * n + 64)
            if 1 <= slot <= 7:
                both = jnp.where(quarter, 1.0, both)
            if slot <= 8:
                here = jnp.where(quarter, 1.0, here)
        wt[blk + 12] = stacked(w * both)
        tmask[blk + 12] = here
    for slot in range(NS):
        rows = jnp.concatenate([gsb[slot], gsp[slot]], axis=1)
        ws[slot] = stacked(weights_of(rows))
        blob_col = gsb[slot].T
        part = gsp[slot].T
        for c in range(3):
            scol[c, slot, 0:128, :] = jnp.broadcast_to(blob_col[:, c : c + 1], (128, 128))
            scol[c, slot, 128:192, :] = jnp.broadcast_to(part[:64, c : c + 1], (64, 128))
            acol[c, slot, :, :] = jnp.broadcast_to(part[:64, c + 3 : c + 4] * -3.0, (64, 128))
    acct[...] = jnp.zeros_like(acct)
    acct5[...] = jnp.zeros_like(acct5)
    accs[...] = jnp.zeros_like(accs)
    accs5[...] = jnp.zeros_like(accs5)

    def values(slot, blk, part, held):
        khi, klo, qhi, qlo, uhi, ulo = held
        def split(x, high, low, rows, cols):
            hi = x.astype(BF16)
            high[rows, cols] = hi
            low[rows, cols] = (x - hi.astype(F32)).astype(BF16)

        half = [slice(0, 128), slice(128, 256)]
        tx = [[jnp.broadcast_to(tr[blk, c : c + 1, cols], (16, 128)) for c in range(3)] for cols in half]
        ta = [[jnp.broadcast_to(tr[blk, c + 3 : c + 4, cols] * 3.0, (16, 128)) for c in range(3)] for cols in half] if part else None
        for g in range(12):
            rows = slice(16 * g, 16 * g + 16)
            sx = [scol[c, slot, rows, :] for c in range(3)]
            if g >= 8:
                part_rows = slice(16 * (g - 8), 16 * (g - 8) + 16)
                sa = [acol[c, slot, part_rows, :] for c in range(3)]
            for h, cols in enumerate(half):
                d = [tx[h][c] - sx[c] for c in range(3)]
                q = (d[0] * d[0] + d[1] * d[1]) + (d[2] * d[2] + SIGMA)
                inv = lax.rsqrt(q)
                inv2 = inv * inv
                k = inv2 * inv
                split(k, khi, klo, rows, cols)
                if part or g >= 8:
                    k5 = k * inv2
                if part:
                    split(k5 * ((ta[h][0] * d[0] + ta[h][1] * d[1]) + ta[h][2] * d[2]), qhi, qlo, rows, cols)
                if g >= 8:
                    split(k5 * ((sa[0] * d[0] + sa[1] * d[1]) + sa[2] * d[2]), uhi, ulo, part_rows, cols)

    def sums(slot, blk, side, part, held):
        khi, klo, qhi, qlo, uhi, ulo = held
        w = ws[slot][:, :192]
        v = wt[blk + 12 * side]
        mask = tmask[blk + 12 * side]
        acct[blk] += (fold3(mm(w, khi[...], NN)) + fold2(mm(w[:16], klo[...], NN))) * mask
        if part:
            acct5[blk - 8] += (fold3(mm(w, qhi[...], NN)) + fold2(mm(w[:16], qlo[...], NN))) * mask
        accs[slot, :, :192] += fold3(mm(v, khi[...], NT)) + fold2(mm(v[:16], klo[...], NT))
        accs5[slot, :, :64] += fold3(mm(v, uhi[...], NT)) + fold2(mm(v[:16], ulo[...], NT))

    held0 = (khi0, klo0, qhi0, qlo0, uhi0, ulo0)
    held1 = (khi1, klo1, qhi1, qlo1, uhi1, ulo1)
    for ref in held1:
        ref[...] = jnp.zeros_like(ref)

    def run(first, per, extra, part):
        main = 7 * per
        zero = jnp.int32(0)

        def step(m, last):
            inner = m < main
            slot = jnp.where(inner, 1 + m // per, 0)
            other = jnp.where(inner, slot, 8)
            blk = first + jnp.where(inner, 2 * lax.rem(m, per), m - main)
            second = jnp.where(inner, blk + 1, blk)
            side = jnp.where(inner, 0, 1)
            values(slot, blk, part, held0)
            sums(*last, part, held1)
            values(other, second, part, held1)
            sums(slot, blk, side, part, held0)
            return (other, second, side)

        last = lax.fori_loop(0, main + extra, step, (zero, zero + first, zero))
        return last

    last = run(0, 4, 5, False)
    sums(*last, False, held1)
    for ref in held1:
        ref[...] = jnp.zeros_like(ref)
    last = run(8, 2, 3, True)
    sums(*last, True, held1)

    def finish(rows, acc, acc5):
        x = [rows[c : c + 1] for c in range(3)]
        a = [rows[c + 3 : c + 4] for c in range(3)]
        sums = [acc[c : c + 1] for c in range(6)]
        vel = [m - n for m, n in zip(cross(x, sums[:3]), sums[3:])]
        if acc5 is None:
            return vel
        sums5 = [acc5[c : c + 1] for c in range(6)]
        turn = cross(a, sums[:3])
        pull = cross(x, sums5[:3])
        return vel + [turn[c] - (pull[c] - sums5[3 + c]) for c in range(3)]

    pad2 = jnp.zeros((2, 256), F32)
    pad5 = jnp.zeros((5, 256), F32)
    for blk in range(12):
        rows = tr[blk]
        if blk < 8:
            out = jnp.concatenate([*finish(rows, acct[blk], None), pad5], axis=0)
            rt[2 * blk, :, 0:128] = out[:, :128]
            rt[2 * blk + 1, :, 0:128] = out[:, 128:]
        else:
            out = jnp.concatenate([*finish(rows, acct[blk], acct5[blk - 8]), pad2], axis=0)
            for h in range(2):
                one, two = PAIRS[2 * (blk - 8) + h]
                half = out[:, 128 * h : 128 * h + 128]
                rt[one, :, 128:256] = half
                rt[two, :, 128:256] = pltpu.roll(half, 64, 1)
    for slot in range(NS):
        rows = jnp.concatenate([gsb[slot], gsp[slot]], axis=1)
        acc = accs[slot]
        vel = finish(rows, acc, None)
        five = accs5[slot]
        full = finish(rows[:, 128:], acc[:, 128:], five)
        rs[slot, :, 0:128] = jnp.concatenate([v[:, :128] for v in vel] + [pad5[:, :128]], axis=0)
        rs[slot, :, 128:256] = jnp.concatenate([*full, pad2[:, :128]], axis=0)

    def t_result(d):
        return pltpu.make_async_remote_copy(rt.at[d], it.at[d - 1], tsend.at[d - 1], trecv.at[d - 1], device_id=on_plane(a + d), device_id_type=MESH)

    def s_result(d):
        return pltpu.make_async_remote_copy(rs.at[d], is_.at[d - 1], ssend.at[d - 1], srecv.at[d - 1], device_id=on_line(b + d), device_id_type=MESH)

    @pl.loop(1, RING)
    def _(d):
        t_result(d).start()

    @pl.loop(1, NS)
    def _(d):
        s_result(d).start()

    @pl.loop(1, RING)
    def _(d):
        t_result(d).wait()

    @pl.loop(1, NS)
    def _(d):
        s_result(d).wait()

    leave.wait()
    total = rt[0] + rs[0]
    for n in range(RING - 1):
        total = total + it[n]
    for n in range(NS - 1):
        total = total + is_[n]
    total = total * -kernel_scale
    slots = rates.shape[1]
    lane = lax.broadcasted_iota(jnp.int32, (6, slots), 1)
    rates[...] = jnp.where(lane < live[0], total[0:6, 128 : 128 + slots], 0.0)
    blob[...] = total[0:3, 0:128]


def per_device(positions, strengths, live_counts, vorticity, diffusivity, seed_counts):
    nx, ny, nz = diffusivity.shape
    vmem = pl.BlockSpec(memory_space=pltpu.VMEM)
    anywhere = pl.BlockSpec(memory_space=pl.ANY)
    dma = pltpu.SemaphoreType.DMA
    return pl.pallas_call(
        step_kernel,
        out_shape=(
            jax.ShapeDtypeStruct(vorticity.shape, F32),
            jax.ShapeDtypeStruct((6, 64), F32),
            jax.ShapeDtypeStruct((3, 128), F32),
        ),
        in_specs=[anywhere] * 5 + [pl.BlockSpec(memory_space=pltpu.SMEM)],
        out_specs=(anywhere, vmem, vmem),
        scratch_shapes=[
            pltpu.VMEM(vorticity.shape, F32),
            pltpu.VMEM(diffusivity.shape, F32),
            pltpu.VMEM(seed_counts.shape, jnp.int32),
            pltpu.VMEM(positions.shape, F32),
            pltpu.VMEM(strengths.shape, F32),
            dma((5,)),
            pltpu.VMEM((2, 3, ny, nz), F32),
            pltpu.VMEM((2, 48, nz), F32),
            pltpu.VMEM((2, 48, nz), F32),
            pltpu.VMEM((8, 128), F32),
            pltpu.VMEM((8, 128), F32),
            pltpu.VMEM((16, 8, 128), F32),
            pltpu.VMEM((16, 8, 128), F32),
            pltpu.VMEM((NS, 8, 128), F32),
            pltpu.VMEM((NS, 8, 128), F32),
            pltpu.VMEM((3, ny, nz), F32),
            pltpu.VMEM((2, ny, nz), F32),
            dma((4,)),
            dma((4,)),
            dma((15,)),
            dma((15,)),
            dma((8,)),
            dma((8,)),
            dma((15,)),
            dma((15,)),
            dma((8,)),
            dma((8,)),
            pltpu.VMEM(vorticity.shape, F32),
            dma,
            pltpu.VMEM((16, 8, 256), F32),
            pltpu.VMEM((NS, 8, 256), F32),
            pltpu.VMEM((12, 8, 256), F32),
            pltpu.VMEM((24, 32, 256), BF16),
            pltpu.VMEM((NS, 32, 256), BF16),
            pltpu.VMEM((3, NS, 192, 128), F32),
            pltpu.VMEM((3, NS, 64, 128), F32),
            pltpu.VMEM((12, 8, 256), F32),
            pltpu.VMEM((4, 8, 256), F32),
            pltpu.VMEM((NS, 8, 256), F32),
            pltpu.VMEM((NS, 8, 128), F32),
            pltpu.VMEM((24, 1, 256), F32),
            *([pltpu.VMEM((192, 256), BF16)] * 4 + [pltpu.VMEM((64, 256), BF16)] * 2) * 2,
            pltpu.VMEM((15, 8, 256), F32),
            pltpu.VMEM((NS - 1, 8, 256), F32),
            dma((15,)),
            dma((15,)),
            dma((NS - 1,)),
            dma((NS - 1,)),
        ],
        compiler_params=pltpu.CompilerParams(vmem_limit_bytes=60 * 1024 * 1024, collective_id=0, has_side_effects=True),
        name="step",
    )(vorticity, diffusivity, seed_counts, positions, strengths, live_counts)


def solution(mesh):
    placed = (
        P(None, ("tgt", "src", "grp")),
        P(None, ("tgt", "src", "grp")),
        P(("tgt", "src", "grp")),
        P(None, "tgt", ("src", "grp"), None),
        P("tgt", ("src", "grp"), None),
        P("tgt", ("src", "grp"), None),
    )
    return jax.shard_map(
        per_device,
        mesh=mesh,
        in_specs=placed,
        out_specs=(
            P(None, "tgt", ("src", "grp"), None),
            P(None, ("tgt", "src", "grp")),
            P(None, ("tgt", "src", "grp")),
        ),
        check_vma=False,
    )
```

```python
import jax
import jax.numpy as jnp
from jax import lax
from jax.experimental import pallas as pl
from jax.experimental.pallas import tpu as pltpu
from jax.sharding import PartitionSpec as P

kernel_scale = 0.25 / 3.141592653589793
seed_weight = 0.0001

SIGMA = 0.0004
F32, BF16 = jnp.float32, jnp.bfloat16
PAIRS = ((0, 8), (1, 2), (3, 4), (5, 6), (7, 9), (10, 11), (12, 13), (14, 15))
NS = 9
COUPLES = ((1, 2), (3, 4), (5, 6), (7, None), (0, 8))


def cross(a, b):
    return (
        a[1] * b[2] - a[2] * b[1],
        a[2] * b[0] - a[0] * b[2],
        a[0] * b[1] - a[1] * b[0],
    )


def pieces(rows):
    one = rows.astype(BF16)
    rest = rows - one.astype(F32)
    two = rest.astype(BF16)
    three = (rest - two.astype(F32)).astype(BF16)
    return one, two, three


def weights_of(rows):
    x = [rows[c : c + 1] for c in range(3)]
    a = [rows[c + 3 : c + 4] for c in range(3)]
    b = cross(x, a)
    zero = jnp.zeros_like(a[0])
    return jnp.concatenate([*a, *b, zero, zero], axis=0)


def stacked(rows):
    one, two, three = pieces(rows)
    return jnp.concatenate([one, two, three, jnp.zeros_like(one)], axis=0)


def fold3(m):
    return m[0:8] + m[8:16] + m[16:24]


def fold2(m):
    return m[0:8] + m[8:16]


NN = (((1,), (0,)), ((), ()))
NT = (((1,), (1,)), ((), ()))


def mm(a, b, dims):
    return lax.dot_general(a, b, dims, preferred_element_type=F32)


MESH = pl.DeviceIdType.MESH
RING = 16


def place():
    tgt, src = lax.axis_index("tgt"), lax.axis_index("src")
    return src * 2 + tgt // 8, lax.rem(tgt, 8) * 2 + lax.axis_index("grp")


def on_plane(a):
    a = lax.rem(a, RING)
    return {"tgt": lax.rem(a, 2) * 8 + lax.rem(lax.axis_index("tgt"), 8), "src": a // 2}


def on_line(b):
    b = lax.rem(b, RING)
    return {"tgt": (lax.axis_index("tgt") // 8) * 8 + b // 2, "grp": lax.rem(b, 2)}


def on_tgt(u):
    return {"tgt": lax.rem(u, RING)}


def on_side(p):
    p = lax.rem(p, RING)
    return {"src": p // 2, "grp": lax.rem(p, 2)}


def step_kernel(vort_in, diff_in, seeds_in, pos_in, stren_in, live, vnext, rates, blob, vort, diff, seeds, pos, stren, local, hx, hy, sy, elp, elb, gtb, gtp, gsb, gsp, gaccs, accw, halo_send, halo_recv, tps, tpr, sps, spr, tbs, tbr, sbs, sbr, vnew, out_sem, rt, rs, tr, wt, ws, scol, acol, acct, acct5, accs, accs5, wp, pcol, pacol, accp, accp5, tmask, khi0, klo0, qhi0, qlo0, uhi0, ulo0, khi1, klo1, qhi1, qlo1, uhi1, ulo1, it, is_, tsend, trecv, ssend, srecv):
    u, p = lax.axis_index("tgt"), lax.axis_index("src") * 2 + lax.axis_index("grp")
    a, b = place()
    fetch = [pltpu.make_async_copy(src, dst, local.at[n]) for n, (src, dst) in enumerate(((pos_in, pos), (stren_in, stren), (vort_in, vort), (diff_in, diff), (seeds_in, seeds)))]
    for copy in fetch:
        copy.start()
    barrier = pltpu.get_barrier_semaphore()
    for to in (on_tgt(u + 1), on_tgt(u + RING - 1), on_side(p + 1), on_side(p + RING - 1)):
        pl.semaphore_signal(barrier, inc=1, device_id=to, device_id_type=MESH)

    @pl.loop(1, RING)
    def _(d):
        pl.semaphore_signal(barrier, inc=1, device_id=on_plane(a + d), device_id_type=MESH)
        pl.semaphore_signal(barrier, inc=1, device_id=on_line(b + d), device_id_type=MESH)

    nx, ny, nz = diff.shape
    fetch[0].wait()
    fetch[1].wait()
    fetch[2].wait()
    for c in range(3):
        sy[0, 16 * c : 16 * c + nx, :] = vort[c, :, 0, :]
        sy[1, 16 * c : 16 * c + nx, :] = vort[c, :, ny - 1, :]
    slots = pos.shape[1]
    elp[...] = jnp.zeros_like(elp)
    elp[0:3, 0:slots] = pos[...]
    lane = lax.broadcasted_iota(jnp.int32, (3, slots), 1)
    elp[3:6, 0:slots] = jnp.where(lane < live[0], stren[...], 0.0)
    pl.semaphore_wait(barrier, 2 * (RING - 1) + 4)

    halos = []
    for n, (src, dst, to) in enumerate(
        (
            (vort.at[:, 0], hx.at[1], on_tgt(u + RING - 1)),
            (vort.at[:, nx - 1], hx.at[0], on_tgt(u + 1)),
            (sy.at[0], hy.at[1], on_side(p + RING - 1)),
            (sy.at[1], hy.at[0], on_side(p + 1)),
        )
    ):
        halos.append(pltpu.make_async_remote_copy(src, dst, halo_send.at[n], halo_recv.at[n], device_id=to, device_id_type=MESH))
    for copy in halos:
        copy.start()

    def tgt_copy(src, held, send, recv, d):
        return pltpu.make_async_remote_copy(src, held.at[RING - d], send.at[d - 1], recv.at[RING - 1 - d], device_id=on_plane(a + d), device_id_type=MESH)

    def side_copy(src, held, send, recv, d):
        return pltpu.make_async_remote_copy(src, held.at[d], send.at[d - 1], recv.at[d - 1], device_id=on_line(b + RING - d), device_id_type=MESH)

    @pl.loop(1, RING)
    def _(d):
        tgt_copy(elp, gtp, tps, tpr, d).start()

    @pl.loop(1, NS)
    def _(d):
        side_copy(elp, gsp, sps, spr, d).start()

    fetch[3].wait()
    fetch[4].wait()
    row = lax.broadcasted_iota(jnp.int32, (ny, nz), 0)
    col = lax.broadcasted_iota(jnp.int32, (ny, nz), 1)
    gaccs[...] = jnp.zeros_like(gaccs)
    accw[...] = jnp.zeros_like(accw)

    def plane(i, low, high):
        counts = seeds[i].astype(F32)
        weight = counts + 1.0
        accw[0] += weight
        accw[1] += weight * jnp.asarray(i, jnp.int32).astype(F32)
        rate = diff[i]
        for c in range(3):
            v = vort[c, i]
            beside = jnp.where(row > 0, pltpu.roll(v, 1, 0), 0.0)
            beside += jnp.where(row < ny - 1, pltpu.roll(v, ny - 1, 0), 0.0)
            beside += jnp.where(col > 0, pltpu.roll(v, 1, 1), 0.0)
            beside += jnp.where(col < nz - 1, pltpu.roll(v, nz - 1, 1), 0.0)
            if low:
                beside += vort[c, i - 1]
            if high:
                beside += vort[c, i + 1]
            new = v + rate * (beside - 6.0 * v)
            vnew[c, i] = new
            gaccs[c] += counts * new

    plane(0, False, True)

    @pl.loop(1, nx - 1)
    def _(i):
        plane(i, True, True)

    plane(nx - 1, True, False)

    for copy in halos:
        copy.wait()
    sides = [
        [(u > 0).astype(F32), (u < RING - 1).astype(F32)],
        [(p > 0).astype(F32), (p < RING - 1).astype(F32)],
    ]
    extra = []
    for end, i in enumerate((0, nx - 1)):
        counts = seeds[i].astype(F32)
        rate = diff[i] * sides[0][end]
        for c in range(3):
            more = rate * hx[end, c]
            vnew[c, i] += more
            gaccs[c] += counts * more
    edge = [jnp.zeros((1, nz), F32) for _ in range(3)]
    for end, j in enumerate((0, ny - 1)):
        counts = seeds[:, j, :].astype(F32)
        rate = diff[:, j, :] * sides[1][end]
        for c in range(3):
            more = rate * hy[end, 16 * c : 16 * c + nx, :]
            vnew[c, :, j, :] = vnew[c, :, j, :] + more
            edge[c] = edge[c] + jnp.sum(counts * more, axis=0, keepdims=True)

    leave = pltpu.make_async_copy(vnew, vnext, out_sem)
    leave.start()
    weight = accw[0]
    odd = jnp.where(lax.rem(col, 2) == 1, weight, 0.0)
    sums = [jnp.sum(gaccs[c], axis=0, keepdims=True) + edge[c] for c in range(3)]
    sums += [jnp.sum(m, axis=0, keepdims=True) for m in (weight, accw[1], weight * row.astype(F32), odd)]
    sums.append(jnp.zeros((1, nz), F32))
    half = (lax.broadcasted_iota(jnp.int32, (nz, nz // 2), 0) // 2 == lax.broadcasted_iota(jnp.int32, (nz, nz // 2), 1)).astype(F32)
    folded = jnp.dot(jnp.concatenate(sums, axis=0), half, precision=lax.Precision.HIGHEST, preferred_element_type=F32)
    total = folded[3:4]
    block = lax.broadcasted_iota(jnp.int32, (1, nz // 2), 1).astype(F32)
    x = ((u * nx).astype(F32) + 0.5 + folded[4:5] / total) / nz
    y = ((p * ny).astype(F32) + 0.5 + folded[5:6] / total) / nz
    z = (2.0 * block + 0.5 + folded[6:7] / total) / nz
    zero = jnp.zeros_like(x)
    elb[...] = jnp.concatenate([x, y, z, *[folded[c : c + 1] * seed_weight for c in range(3)], zero, zero], axis=0)

    @pl.loop(1, RING)
    def _(d):
        tgt_copy(elb, gtb, tbs, tbr, d).start()

    @pl.loop(1, NS)
    def _(d):
        side_copy(elb, gsb, sbs, sbr, d).start()

    gtb[0] = elb[...]
    gsb[0] = elb[...]
    gtp[0] = elp[...]
    gsp[0] = elp[...]

    @pl.loop(1, RING)
    def _(d):
        tgt_copy(elp, gtp, tps, tpr, d).wait()

    @pl.loop(1, NS)
    def _(d):
        side_copy(elp, gsp, sps, spr, d).wait()

    lane = lax.broadcasted_iota(jnp.int32, (8, 128), 1)
    lane2 = lax.broadcasted_iota(jnp.int32, (1, 256), 1)
    def target_block(blk):
        if blk < 8:
            halves = [gtb[2 * blk], gtb[2 * blk + 1]]
            slots = [2 * blk, 2 * blk, 2 * blk + 1, 2 * blk + 1]
        else:
            slots = [s for h in range(2) for s in PAIRS[2 * (blk - 8) + h]]
            halves = [jnp.where(lane < 64, gtp[one], pltpu.roll(gtp[two], 64, 1)) for one, two in (slots[:2], slots[2:])]
        rows = jnp.concatenate(halves, axis=1)
        tr[blk] = rows
        w = weights_of(rows)
        wt[blk] = stacked(w)
        tmask[blk] = jnp.ones((1, 256), F32)
        both = jnp.zeros((1, 256), F32)
        here = jnp.zeros((1, 256), F32)
        for n, slot in enumerate(slots):
            quarter = (lane2 >= 64 * n) & (lane2 < 64 * n + 64)
            if 1 <= slot <= 7:
                both = jnp.where(quarter, 1.0, both)
            if slot <= 8:
                here = jnp.where(quarter, 1.0, here)
        wt[blk + 12] = stacked(w * both)
        tmask[blk + 12] = here

    for blk in range(8, 12):
        target_block(blk)
    for n, (one, two) in enumerate(COUPLES):
        second = 0.0 if two is None else pltpu.roll(gsp[two], 64, 1)
        couple = jnp.where(lane < 64, gsp[one], second)
        wp[n] = stacked(weights_of(couple))
        across = couple.T
        for c in range(3):
            spread = jnp.broadcast_to(across[:, c : c + 1], (128, 128))
            turn = jnp.broadcast_to(across[:, c + 3 : c + 4] * -3.0, (128, 128))
            pcol[c, n] = spread
            pacol[c, n] = turn
            scol[c, one, 128:192, :] = spread[:64]
            acol[c, one] = turn[:64]
            if two is not None:
                scol[c, two, 128:192, :] = spread[64:]
                acol[c, two] = turn[64:]
    for ref in (acct, acct5, accs, accs5, accp, accp5):
        ref[...] = jnp.zeros_like(ref)

    def split(x, high, low, rows, cols):
        hi = x.astype(BF16)
        high[rows, cols] = hi
        low[rows, cols] = (x - hi.astype(F32)).astype(BF16)

    WIDE = 4

    def values(kind, slot, blk, held):
        khi, klo, qhi, qlo, uhi, ulo = held

        def row(c, h):
            return tr[blk + h // 2, c : c + 1, 128 * (h % 2) : 128 * (h % 2) + 128]

        for pair in range(WIDE // 2):
            lanes = range(2 * pair, 2 * pair + 2)
            tx = {h: [jnp.broadcast_to(row(c, h), (16, 128)) for c in range(3)] for h in lanes}
            if kind != "b":
                ta = {h: [jnp.broadcast_to(row(c + 3, h) * 3.0, (16, 128)) for c in range(3)] for h in lanes}
            for g in range(12 if kind == "b" else 8):
                rows = slice(16 * g, 16 * g + 16)
                turned = kind == "p" or g >= 8
                if kind == "p":
                    sx = [pcol[c, slot, rows, :] for c in range(3)]
                    sa = [pacol[c, slot, rows, :] for c in range(3)]
                    part_rows = rows
                else:
                    sx = [scol[c, slot, rows, :] for c in range(3)]
                    if turned:
                        part_rows = slice(16 * (g - 8), 16 * (g - 8) + 16)
                        sa = [acol[c, slot, part_rows, :] for c in range(3)]
                for h in lanes:
                    cols = slice(128 * h, 128 * h + 128)
                    d = [tx[h][c] - sx[c] for c in range(3)]
                    q = (d[0] * d[0] + d[1] * d[1]) + (d[2] * d[2] + SIGMA)
                    inv = lax.rsqrt(q)
                    inv2 = inv * inv
                    k = inv2 * inv
                    split(k, khi, klo, rows, cols)
                    if kind != "b" or turned:
                        k5 = k * inv2
                    if kind != "b":
                        split(k5 * ((ta[h][0] * d[0] + ta[h][1] * d[1]) + ta[h][2] * d[2]), qhi, qlo, rows, cols)
                    if turned:
                        split(k5 * ((sa[0] * d[0] + sa[1] * d[1]) + sa[2] * d[2]), uhi, ulo, part_rows, cols)

    def sums(kind, slot, blk, side, held):
        khi, klo, qhi, qlo, uhi, ulo = held
        which = [blk + 12 * side + n for n in range(WIDE // 2)]
        v = jnp.concatenate([wt[n] for n in which], axis=1)
        if kind == "b":
            w = ws[slot][:, :192]
        elif kind == "m":
            w = ws[slot][:, :128]
        else:
            w = wp[slot]
        n = w.shape[1]

        def down(high, low):
            return fold3(mm(w, high[:n], NN)) + fold2(mm(w[:16], low[:n], NN))

        def over(high, low, m):
            return fold3(mm(v, high[:m], NT)) + fold2(mm(v[:16], low[:m], NT))

        first = down(khi, klo)
        for j, m in enumerate(which):
            acct[blk + j] += first[:, 256 * j : 256 * j + 256] * tmask[m]
        if kind != "b":
            first = down(qhi, qlo)
            for j, m in enumerate(which):
                acct5[blk + j - 8] += first[:, 256 * j : 256 * j + 256] * tmask[m]
        if kind == "p":
            accp[slot] += over(khi, klo, 128)
            accp5[slot] += over(uhi, ulo, 128)
        else:
            accs[slot, :, :n] += over(khi, klo, n)
        if kind == "b":
            accs5[slot, :, :64] += over(uhi, ulo, 64)

    held0 = (khi0, klo0, qhi0, qlo0, uhi0, ulo0)
    held1 = (khi1, klo1, qhi1, qlo1, uhi1, ulo1)
    def run(kind, first, per, main, extra, place_of):
        for ref in held1:
            ref[...] = jnp.zeros_like(ref)
        zero = jnp.int32(0)

        def step(m, last):
            one, two = place_of(m, m < main, first, per, main)
            values(kind, one[0], one[1], held0)
            sums(kind, *last, held1)
            values(kind, two[0], two[1], held1)
            sums(kind, *one, held0)
            return two

        last = lax.fori_loop(0, main + extra, step, (zero, zero + first, zero))
        sums(kind, *last, held1)

    def blob_place(m, inner, first, per, main):
        slot = jnp.where(inner, 1 + m // per, 0)
        blk = jnp.where(inner, 4 * lax.rem(m, per), 2 * (m - main))
        side = jnp.where(inner, 0, 1)
        return (slot, blk, side), (jnp.where(inner, slot, 8), jnp.where(inner, blk + 2, blk), side)

    def mixed_place(m, inner, first, per, main):
        slot = jnp.where(inner, m + 1, 8 * (m - main))
        side = jnp.where(inner, 0, 1)
        return (slot, jnp.int32(8), side), (slot, jnp.int32(10), side)

    def couple_place(m, inner, first, per, main):
        side = jnp.where(inner, 0, 1)
        return (m, jnp.int32(8), side), (m, jnp.int32(10), side)

    run("p", 8, 1, 4, 1, couple_place)
    @pl.loop(1, RING)
    def _(d):
        tgt_copy(elb, gtb, tbs, tbr, d).wait()

    @pl.loop(1, NS)
    def _(d):
        side_copy(elb, gsb, sbs, sbr, d).wait()

    for blk in range(8):
        target_block(blk)
    for slot in range(NS):
        ws[slot] = stacked(weights_of(jnp.concatenate([gsb[slot], gsp[slot]], axis=1)))
        across = gsb[slot].T
        for c in range(3):
            scol[c, slot, 0:128, :] = jnp.broadcast_to(across[:, c : c + 1], (128, 128))
    run("b", 0, 2, 14, 3, blob_place)
    run("m", 8, 1, 7, 2, mixed_place)

    def finish(rows, acc, acc5):
        x = [rows[c : c + 1] for c in range(3)]
        a = [rows[c + 3 : c + 4] for c in range(3)]
        sums = [acc[c : c + 1] for c in range(6)]
        vel = [m - n for m, n in zip(cross(x, sums[:3]), sums[3:])]
        if acc5 is None:
            return vel
        sums5 = [acc5[c : c + 1] for c in range(6)]
        turn = cross(a, sums[:3])
        pull = cross(x, sums5[:3])
        return vel + [turn[c] - (pull[c] - sums5[3 + c]) for c in range(3)]

    pad2 = jnp.zeros((2, 256), F32)
    pad5 = jnp.zeros((5, 256), F32)
    for blk in range(12):
        rows = tr[blk]
        if blk < 8:
            out = jnp.concatenate([*finish(rows, acct[blk], None), pad5], axis=0)
            rt[2 * blk, :, 0:128] = out[:, :128]
            rt[2 * blk + 1, :, 0:128] = out[:, 128:]
        else:
            out = jnp.concatenate([*finish(rows, acct[blk], acct5[blk - 8]), pad2], axis=0)
            for h in range(2):
                one, two = PAIRS[2 * (blk - 8) + h]
                half = out[:, 128 * h : 128 * h + 128]
                rt[one, :, 128:256] = half
                rt[two, :, 128:256] = pltpu.roll(half, 64, 1)
    for n, (one, two) in enumerate(COUPLES):
        for slot, back in ((one, False), (two, True)):
            if slot is None:
                continue
            more = [accp[n], accp5[n]]
            if back:
                more = [pltpu.roll(v, 64, 1) for v in more]
            blob_part = finish(gsb[slot], accs[slot, :, :128], None)
            full = finish(gsp[slot], accs[slot, :, 128:] + more[0], accs5[slot] + more[1])
            rs[slot, :, 0:128] = jnp.concatenate([*blob_part, pad5[:, :128]], axis=0)
            rs[slot, :, 128:256] = jnp.concatenate([*full, pad2[:, :128]], axis=0)

    def t_result(d):
        return pltpu.make_async_remote_copy(rt.at[d], it.at[d - 1], tsend.at[d - 1], trecv.at[d - 1], device_id=on_plane(a + d), device_id_type=MESH)

    def s_result(d):
        return pltpu.make_async_remote_copy(rs.at[d], is_.at[d - 1], ssend.at[d - 1], srecv.at[d - 1], device_id=on_line(b + d), device_id_type=MESH)

    @pl.loop(1, RING)
    def _(d):
        t_result(d).start()

    @pl.loop(1, NS)
    def _(d):
        s_result(d).start()

    @pl.loop(1, RING)
    def _(d):
        t_result(d).wait()

    @pl.loop(1, NS)
    def _(d):
        s_result(d).wait()

    leave.wait()
    total = rt[0] + rs[0]
    for n in range(RING - 1):
        total = total + it[n]
    for n in range(NS - 1):
        total = total + is_[n]
    total = total * -kernel_scale
    slots = rates.shape[1]
    lane = lax.broadcasted_iota(jnp.int32, (6, slots), 1)
    rates[...] = jnp.where(lane < live[0], total[0:6, 128 : 128 + slots], 0.0)
    blob[...] = total[0:3, 0:128]


def emit_kernel(grid, rates, blob, grid_out, rates_out, blob_out, held, rates_held, blob_held, come, go):
    ways = [(grid.at[c], held.at[c], grid_out.at[c]) for c in range(3)]
    ways += [(rates, rates_held, rates_out), (blob, blob_held, blob_out)]
    copies = [(pltpu.make_async_copy(a, b, come.at[n]), pltpu.make_async_copy(b, c, go.at[n])) for n, (a, b, c) in enumerate(ways)]
    for first, _ in copies:
        first.start()
    for first, second in copies:
        first.wait()
        second.start()
    for _, second in copies:
        second.wait()


def emit(*arrays):
    anywhere = pl.BlockSpec(memory_space=pl.ANY)
    return pl.pallas_call(
        emit_kernel,
        out_shape=tuple(jax.ShapeDtypeStruct(v.shape, v.dtype) for v in arrays),
        in_specs=[anywhere] * len(arrays),
        out_specs=(anywhere,) * len(arrays),
        scratch_shapes=[*[pltpu.VMEM(v.shape, v.dtype) for v in arrays], pltpu.SemaphoreType.DMA((5,)), pltpu.SemaphoreType.DMA((5,))],
        compiler_params=pltpu.CompilerParams(vmem_limit_bytes=60 * 1024 * 1024),
        name="emit",
    )(*arrays)


def per_device(positions, strengths, live_counts, vorticity, diffusivity, seed_counts):
    nx, ny, nz = diffusivity.shape
    vmem = pl.BlockSpec(memory_space=pltpu.VMEM)
    anywhere = pl.BlockSpec(memory_space=pl.ANY)
    dma = pltpu.SemaphoreType.DMA
    results = pl.pallas_call(
        step_kernel,
        out_shape=(
            jax.ShapeDtypeStruct(vorticity.shape, F32),
            jax.ShapeDtypeStruct((6, 64), F32),
            jax.ShapeDtypeStruct((3, 128), F32),
        ),
        in_specs=[anywhere] * 5 + [pl.BlockSpec(memory_space=pltpu.SMEM)],
        out_specs=(anywhere, vmem, vmem),
        scratch_shapes=[
            pltpu.VMEM(vorticity.shape, F32),
            pltpu.VMEM(diffusivity.shape, F32),
            pltpu.VMEM(seed_counts.shape, jnp.int32),
            pltpu.VMEM(positions.shape, F32),
            pltpu.VMEM(strengths.shape, F32),
            dma((5,)),
            pltpu.VMEM((2, 3, ny, nz), F32),
            pltpu.VMEM((2, 48, nz), F32),
            pltpu.VMEM((2, 48, nz), F32),
            pltpu.VMEM((8, 128), F32),
            pltpu.VMEM((8, 128), F32),
            pltpu.VMEM((16, 8, 128), F32),
            pltpu.VMEM((16, 8, 128), F32),
            pltpu.VMEM((NS, 8, 128), F32),
            pltpu.VMEM((NS, 8, 128), F32),
            pltpu.VMEM((3, ny, nz), F32),
            pltpu.VMEM((2, ny, nz), F32),
            dma((4,)),
            dma((4,)),
            dma((15,)),
            dma((15,)),
            dma((8,)),
            dma((8,)),
            dma((15,)),
            dma((15,)),
            dma((8,)),
            dma((8,)),
            pltpu.VMEM(vorticity.shape, F32),
            dma,
            pltpu.VMEM((16, 8, 256), F32),
            pltpu.VMEM((NS, 8, 256), F32),
            pltpu.VMEM((12, 8, 256), F32),
            pltpu.VMEM((24, 32, 256), BF16),
            pltpu.VMEM((NS, 32, 256), BF16),
            pltpu.VMEM((3, NS, 192, 128), F32),
            pltpu.VMEM((3, NS, 64, 128), F32),
            pltpu.VMEM((12, 8, 256), F32),
            pltpu.VMEM((4, 8, 256), F32),
            pltpu.VMEM((NS, 8, 256), F32),
            pltpu.VMEM((NS, 8, 128), F32),
            pltpu.VMEM((5, 32, 128), BF16),
            pltpu.VMEM((3, 5, 128, 128), F32),
            pltpu.VMEM((3, 5, 128, 128), F32),
            pltpu.VMEM((5, 8, 128), F32),
            pltpu.VMEM((5, 8, 128), F32),
            pltpu.VMEM((24, 1, 256), F32),
            *([pltpu.VMEM((192, 512), BF16)] * 2 + [pltpu.VMEM((128, 512), BF16)] * 4) * 2,
            pltpu.VMEM((15, 8, 256), F32),
            pltpu.VMEM((NS - 1, 8, 256), F32),
            dma((15,)),
            dma((15,)),
            dma((NS - 1,)),
            dma((NS - 1,)),
        ],
        compiler_params=pltpu.CompilerParams(vmem_limit_bytes=60 * 1024 * 1024, collective_id=0, has_side_effects=True),
        name="step",
    )(vorticity, diffusivity, seed_counts, positions, strengths, live_counts)
    return emit(*results)


def solution(mesh):
    placed = (
        P(None, ("tgt", "src", "grp")),
        P(None, ("tgt", "src", "grp")),
        P(("tgt", "src", "grp")),
        P(None, "tgt", ("src", "grp"), None),
        P("tgt", ("src", "grp"), None),
        P("tgt", ("src", "grp"), None),
    )
    return jax.shard_map(
        per_device,
        mesh=mesh,
        in_specs=placed,
        out_specs=(
            P(None, "tgt", ("src", "grp"), None),
            P(None, ("tgt", "src", "grp")),
            P(None, ("tgt", "src", "grp")),
        ),
        check_vma=False,
    )
```

```python
import jax
import jax.numpy as jnp
from jax import lax
from jax.experimental import pallas as pl
from jax.experimental.pallas import tpu as pltpu
from jax.sharding import PartitionSpec as P

kernel_scale = 0.25 / 3.141592653589793
seed_weight = 0.0001

SIGMA = 0.0004
F32, BF16 = jnp.float32, jnp.bfloat16
PAIRS = ((0, 8), (1, 2), (3, 4), (5, 6), (7, 9), (10, 11), (12, 13), (14, 15))
NS = 9
COUPLES = ((1, 2), (3, 4), (5, 6), (7, None), (0, 8))


def cross(a, b):
    return (
        a[1] * b[2] - a[2] * b[1],
        a[2] * b[0] - a[0] * b[2],
        a[0] * b[1] - a[1] * b[0],
    )


def pieces(rows):
    one = rows.astype(BF16)
    rest = rows - one.astype(F32)
    two = rest.astype(BF16)
    three = (rest - two.astype(F32)).astype(BF16)
    return one, two, three


def weights_of(rows):
    x = [rows[c : c + 1] for c in range(3)]
    a = [rows[c + 3 : c + 4] for c in range(3)]
    b = cross(x, a)
    zero = jnp.zeros_like(a[0])
    return jnp.concatenate([*a, *b, zero, zero], axis=0)


def stacked(rows):
    one, two, three = pieces(rows)
    return jnp.concatenate([one, two, three, jnp.zeros_like(one)], axis=0)


def fold3(m):
    return m[0:8] + m[8:16] + m[16:24]


def fold2(m):
    return m[0:8] + m[8:16]


NN = (((1,), (0,)), ((), ()))
NT = (((1,), (1,)), ((), ()))


def mm(a, b, dims):
    return lax.dot_general(a, b, dims, preferred_element_type=F32)


MESH = pl.DeviceIdType.MESH
RING = 16


def place():
    tgt, src = lax.axis_index("tgt"), lax.axis_index("src")
    return src * 2 + tgt // 8, lax.rem(tgt, 8) * 2 + lax.axis_index("grp")


def on_plane(a):
    a = lax.rem(a, RING)
    return {"tgt": lax.rem(a, 2) * 8 + lax.rem(lax.axis_index("tgt"), 8), "src": a // 2}


def on_line(b):
    b = lax.rem(b, RING)
    return {"tgt": (lax.axis_index("tgt") // 8) * 8 + b // 2, "grp": lax.rem(b, 2)}


def on_tgt(u):
    return {"tgt": lax.rem(u, RING)}


def on_side(p):
    p = lax.rem(p, RING)
    return {"src": p // 2, "grp": lax.rem(p, 2)}


def step_kernel(vort_in, diff_in, seeds_in, pos_in, stren_in, live, vnext, rates, blob, vort, diff, seeds, pos, stren, local, hx, hy, sy, elp, elb, gtb, gtp, gsb, gsp, gaccs, accw, halo_send, halo_recv, tps, tpr, sps, spr, tbs, tbr, sbs, sbr, vnew, out_sem, rt, rs, tr, wt, ws, scol, acol, acct, acct5, accs, accs5, wp, pcol, pacol, accp, accp5, tmask, khi0, klo0, qhi0, qlo0, uhi0, ulo0, khi1, klo1, qhi1, qlo1, uhi1, ulo1, it, is_, tsend, trecv, ssend, srecv):
    u, p = lax.axis_index("tgt"), lax.axis_index("src") * 2 + lax.axis_index("grp")
    a, b = place()
    fetch = [pltpu.make_async_copy(src, dst, local.at[n]) for n, (src, dst) in enumerate(((pos_in, pos), (stren_in, stren), (vort_in, vort), (diff_in, diff), (seeds_in, seeds)))]
    for copy in fetch:
        copy.start()
    barrier = pltpu.get_barrier_semaphore()
    for to in (on_tgt(u + 1), on_tgt(u + RING - 1), on_side(p + 1), on_side(p + RING - 1)):
        pl.semaphore_signal(barrier, inc=1, device_id=to, device_id_type=MESH)

    @pl.loop(1, RING)
    def _(d):
        pl.semaphore_signal(barrier, inc=1, device_id=on_plane(a + d), device_id_type=MESH)
        pl.semaphore_signal(barrier, inc=1, device_id=on_line(b + d), device_id_type=MESH)

    nx, ny, nz = diff.shape
    fetch[0].wait()
    fetch[1].wait()
    fetch[2].wait()
    for c in range(3):
        sy[0, 16 * c : 16 * c + nx, :] = vort[c, :, 0, :]
        sy[1, 16 * c : 16 * c + nx, :] = vort[c, :, ny - 1, :]
    slots = pos.shape[1]
    elp[...] = jnp.zeros_like(elp)
    elp[0:3, 0:slots] = pos[...]
    lane = lax.broadcasted_iota(jnp.int32, (3, slots), 1)
    elp[3:6, 0:slots] = jnp.where(lane < live[0], stren[...], 0.0)
    pl.semaphore_wait(barrier, 2 * (RING - 1) + 4)

    halos = []
    for n, (src, dst, to) in enumerate(
        (
            (vort.at[:, 0], hx.at[1], on_tgt(u + RING - 1)),
            (vort.at[:, nx - 1], hx.at[0], on_tgt(u + 1)),
            (sy.at[0], hy.at[1], on_side(p + RING - 1)),
            (sy.at[1], hy.at[0], on_side(p + 1)),
        )
    ):
        halos.append(pltpu.make_async_remote_copy(src, dst, halo_send.at[n], halo_recv.at[n], device_id=to, device_id_type=MESH))
    for copy in halos:
        copy.start()

    def tgt_copy(src, held, send, recv, d):
        return pltpu.make_async_remote_copy(src, held.at[RING - d], send.at[d - 1], recv.at[RING - 1 - d], device_id=on_plane(a + d), device_id_type=MESH)

    def side_copy(src, held, send, recv, d):
        return pltpu.make_async_remote_copy(src, held.at[d], send.at[d - 1], recv.at[d - 1], device_id=on_line(b + RING - d), device_id_type=MESH)

    @pl.loop(1, RING)
    def _(d):
        tgt_copy(elp, gtp, tps, tpr, d).start()

    @pl.loop(1, NS)
    def _(d):
        side_copy(elp, gsp, sps, spr, d).start()

    fetch[3].wait()
    fetch[4].wait()
    row = lax.broadcasted_iota(jnp.int32, (ny, nz), 0)
    col = lax.broadcasted_iota(jnp.int32, (ny, nz), 1)
    gaccs[...] = jnp.zeros_like(gaccs)
    accw[...] = jnp.zeros_like(accw)

    def plane(i, low, high):
        counts = seeds[i].astype(F32)
        weight = counts + 1.0
        accw[0] += weight
        accw[1] += weight * jnp.asarray(i, jnp.int32).astype(F32)
        rate = diff[i]
        for c in range(3):
            v = vort[c, i]
            beside = jnp.where(row > 0, pltpu.roll(v, 1, 0), 0.0)
            beside += jnp.where(row < ny - 1, pltpu.roll(v, ny - 1, 0), 0.0)
            beside += jnp.where(col > 0, pltpu.roll(v, 1, 1), 0.0)
            beside += jnp.where(col < nz - 1, pltpu.roll(v, nz - 1, 1), 0.0)
            if low:
                beside += vort[c, i - 1]
            if high:
                beside += vort[c, i + 1]
            new = v + rate * (beside - 6.0 * v)
            vnew[c, i] = new
            gaccs[c] += counts * new

    plane(0, False, True)

    @pl.loop(1, nx - 1)
    def _(i):
        plane(i, True, True)

    plane(nx - 1, True, False)

    for copy in halos:
        copy.wait()
    sides = [
        [(u > 0).astype(F32), (u < RING - 1).astype(F32)],
        [(p > 0).astype(F32), (p < RING - 1).astype(F32)],
    ]
    extra = []
    for end, i in enumerate((0, nx - 1)):
        counts = seeds[i].astype(F32)
        rate = diff[i] * sides[0][end]
        for c in range(3):
            more = rate * hx[end, c]
            vnew[c, i] += more
            gaccs[c] += counts * more
    edge = [jnp.zeros((1, nz), F32) for _ in range(3)]
    for end, j in enumerate((0, ny - 1)):
        counts = seeds[:, j, :].astype(F32)
        rate = diff[:, j, :] * sides[1][end]
        for c in range(3):
            more = rate * hy[end, 16 * c : 16 * c + nx, :]
            vnew[c, :, j, :] = vnew[c, :, j, :] + more
            edge[c] = edge[c] + jnp.sum(counts * more, axis=0, keepdims=True)

    leave = pltpu.make_async_copy(vnew, vnext, out_sem)
    leave.start()
    weight = accw[0]
    odd = jnp.where(lax.rem(col, 2) == 1, weight, 0.0)
    sums = [jnp.sum(gaccs[c], axis=0, keepdims=True) + edge[c] for c in range(3)]
    sums += [jnp.sum(m, axis=0, keepdims=True) for m in (weight, accw[1], weight * row.astype(F32), odd)]
    sums.append(jnp.zeros((1, nz), F32))
    half = (lax.broadcasted_iota(jnp.int32, (nz, nz // 2), 0) // 2 == lax.broadcasted_iota(jnp.int32, (nz, nz // 2), 1)).astype(F32)
    folded = jnp.dot(jnp.concatenate(sums, axis=0), half, precision=lax.Precision.HIGHEST, preferred_element_type=F32)
    total = folded[3:4]
    block = lax.broadcasted_iota(jnp.int32, (1, nz // 2), 1).astype(F32)
    x = ((u * nx).astype(F32) + 0.5 + folded[4:5] / total) / nz
    y = ((p * ny).astype(F32) + 0.5 + folded[5:6] / total) / nz
    z = (2.0 * block + 0.5 + folded[6:7] / total) / nz
    zero = jnp.zeros_like(x)
    elb[...] = jnp.concatenate([x, y, z, *[folded[c : c + 1] * seed_weight for c in range(3)], zero, zero], axis=0)

    @pl.loop(1, RING)
    def _(d):
        tgt_copy(elb, gtb, tbs, tbr, d).start()

    @pl.loop(1, NS)
    def _(d):
        side_copy(elb, gsb, sbs, sbr, d).start()

    gtb[0] = elb[...]
    gsb[0] = elb[...]
    gtp[0] = elp[...]
    gsp[0] = elp[...]

    @pl.loop(1, RING)
    def _(d):
        tgt_copy(elp, gtp, tps, tpr, d).wait()

    @pl.loop(1, NS)
    def _(d):
        side_copy(elp, gsp, sps, spr, d).wait()

    lane = lax.broadcasted_iota(jnp.int32, (8, 128), 1)
    lane2 = lax.broadcasted_iota(jnp.int32, (1, 256), 1)
    def target_block(blk):
        if blk < 8:
            halves = [gtb[2 * blk], gtb[2 * blk + 1]]
            slots = [2 * blk, 2 * blk, 2 * blk + 1, 2 * blk + 1]
        else:
            slots = [s for h in range(2) for s in PAIRS[2 * (blk - 8) + h]]
            halves = [jnp.where(lane < 64, gtp[one], pltpu.roll(gtp[two], 64, 1)) for one, two in (slots[:2], slots[2:])]
        rows = jnp.concatenate(halves, axis=1)
        tr[blk] = rows
        w = weights_of(rows)
        wt[blk] = stacked(w)
        tmask[blk] = jnp.ones((1, 256), F32)
        both = jnp.zeros((1, 256), F32)
        here = jnp.zeros((1, 256), F32)
        for n, slot in enumerate(slots):
            quarter = (lane2 >= 64 * n) & (lane2 < 64 * n + 64)
            if 1 <= slot <= 7:
                both = jnp.where(quarter, 1.0, both)
            if slot <= 8:
                here = jnp.where(quarter, 1.0, here)
        wt[blk + 12] = stacked(w * both)
        tmask[blk + 12] = here

    for blk in range(8, 12):
        target_block(blk)
    for n, (one, two) in enumerate(COUPLES):
        second = 0.0 if two is None else pltpu.roll(gsp[two], 64, 1)
        couple = jnp.where(lane < 64, gsp[one], second)
        wp[n] = stacked(weights_of(couple))
        across = couple.T
        for c in range(3):
            spread = jnp.broadcast_to(across[:, c : c + 1], (128, 128))
            turn = jnp.broadcast_to(across[:, c + 3 : c + 4] * -3.0, (128, 128))
            pcol[c, n] = spread
            pacol[c, n] = turn
            scol[c, one, 128:192, :] = spread[:64]
            acol[c, one] = turn[:64]
            if two is not None:
                scol[c, two, 128:192, :] = spread[64:]
                acol[c, two] = turn[64:]
    for ref in (acct, acct5, accs, accs5, accp, accp5):
        ref[...] = jnp.zeros_like(ref)

    def split(x, high, low, rows, cols):
        hi = x.astype(BF16)
        high[rows, cols] = hi
        low[rows, cols] = (x - hi.astype(F32)).astype(BF16)

    WIDE = 4

    def values(kind, slot, blk, held):
        khi, klo, qhi, qlo, uhi, ulo = held

        def row(c, h):
            return tr[blk + h // 2, c : c + 1, 128 * (h % 2) : 128 * (h % 2) + 128]

        for pair in range(WIDE // 2):
            lanes = range(2 * pair, 2 * pair + 2)
            tx = {h: [jnp.broadcast_to(row(c, h), (16, 128)) for c in range(3)] for h in lanes}
            if kind != "b":
                ta = {h: [jnp.broadcast_to(row(c + 3, h) * 3.0, (16, 128)) for c in range(3)] for h in lanes}
            for g in range(12 if kind == "b" else 8):
                rows = slice(16 * g, 16 * g + 16)
                turned = kind == "p" or g >= 8
                if kind == "p":
                    sx = [pcol[c, slot, rows, :] for c in range(3)]
                    sa = [pacol[c, slot, rows, :] for c in range(3)]
                    part_rows = rows
                else:
                    sx = [scol[c, slot, rows, :] for c in range(3)]
                    if turned:
                        part_rows = slice(16 * (g - 8), 16 * (g - 8) + 16)
                        sa = [acol[c, slot, part_rows, :] for c in range(3)]
                for h in lanes:
                    cols = slice(128 * h, 128 * h + 128)
                    d = [tx[h][c] - sx[c] for c in range(3)]
                    q = (d[0] * d[0] + d[1] * d[1]) + (d[2] * d[2] + SIGMA)
                    inv = lax.rsqrt(q)
                    inv2 = inv * inv
                    k = inv2 * inv
                    split(k, khi, klo, rows, cols)
                    if kind != "b" or turned:
                        k5 = k * inv2
                    if kind != "b":
                        split(k5 * ((ta[h][0] * d[0] + ta[h][1] * d[1]) + ta[h][2] * d[2]), qhi, qlo, rows, cols)
                    if turned:
                        split(k5 * ((sa[0] * d[0] + sa[1] * d[1]) + sa[2] * d[2]), uhi, ulo, part_rows, cols)

    def sums(kind, slot, blk, side, held):
        khi, klo, qhi, qlo, uhi, ulo = held
        which = [blk + 12 * side + n for n in range(WIDE // 2)]
        v = jnp.concatenate([wt[n] for n in which], axis=1)
        if kind == "b":
            w = ws[slot][:, :192]
        elif kind == "m":
            w = ws[slot][:, :128]
        else:
            w = wp[slot]
        n = w.shape[1]

        def down(high, low):
            return fold3(mm(w, high[:n], NN)) + fold2(mm(w[:16], low[:n], NN))

        def over(high, low, m):
            return fold3(mm(v, high[:m], NT)) + fold2(mm(v[:16], low[:m], NT))

        first = down(khi, klo)
        for j, m in enumerate(which):
            acct[blk + j] += first[:, 256 * j : 256 * j + 256] * tmask[m]
        if kind != "b":
            first = down(qhi, qlo)
            for j, m in enumerate(which):
                acct5[blk + j - 8] += first[:, 256 * j : 256 * j + 256] * tmask[m]
        if kind == "p":
            accp[slot] += over(khi, klo, 128)
            accp5[slot] += over(uhi, ulo, 128)
        else:
            accs[slot, :, :n] += over(khi, klo, n)
        if kind == "b":
            accs5[slot, :, :64] += over(uhi, ulo, 64)

    held0 = (khi0, klo0, qhi0, qlo0, uhi0, ulo0)
    held1 = (khi1, klo1, qhi1, qlo1, uhi1, ulo1)
    def run(kind, first, per, main, extra, place_of):
        for ref in held1:
            ref[...] = jnp.zeros_like(ref)
        zero = jnp.int32(0)

        def step(m, last):
            one, two = place_of(m, m < main, first, per, main)
            values(kind, one[0], one[1], held0)
            sums(kind, *last, held1)
            values(kind, two[0], two[1], held1)
            sums(kind, *one, held0)
            return two

        last = lax.fori_loop(0, main + extra, step, (zero, zero + first, zero), unroll=3)
        sums(kind, *last, held1)

    def blob_place(m, inner, first, per, main):
        slot = jnp.where(inner, 1 + m // per, 0)
        blk = jnp.where(inner, 4 * lax.rem(m, per), 2 * (m - main))
        side = jnp.where(inner, 0, 1)
        return (slot, blk, side), (jnp.where(inner, slot, 8), jnp.where(inner, blk + 2, blk), side)

    def mixed_place(m, inner, first, per, main):
        slot = jnp.where(inner, m + 1, 8 * (m - main))
        side = jnp.where(inner, 0, 1)
        return (slot, jnp.int32(8), side), (slot, jnp.int32(10), side)

    def couple_place(m, inner, first, per, main):
        side = jnp.where(inner, 0, 1)
        return (m, jnp.int32(8), side), (m, jnp.int32(10), side)

    run("p", 8, 1, 4, 1, couple_place)
    @pl.loop(1, RING)
    def _(d):
        tgt_copy(elb, gtb, tbs, tbr, d).wait()

    @pl.loop(1, NS)
    def _(d):
        side_copy(elb, gsb, sbs, sbr, d).wait()

    for blk in range(8):
        target_block(blk)
    for slot in range(NS):
        ws[slot] = stacked(weights_of(jnp.concatenate([gsb[slot], gsp[slot]], axis=1)))
        across = gsb[slot].T
        for c in range(3):
            scol[c, slot, 0:128, :] = jnp.broadcast_to(across[:, c : c + 1], (128, 128))
    run("b", 0, 2, 14, 3, blob_place)
    run("m", 8, 1, 7, 2, mixed_place)

    def finish(rows, acc, acc5):
        x = [rows[c : c + 1] for c in range(3)]
        a = [rows[c + 3 : c + 4] for c in range(3)]
        sums = [acc[c : c + 1] for c in range(6)]
        vel = [m - n for m, n in zip(cross(x, sums[:3]), sums[3:])]
        if acc5 is None:
            return vel
        sums5 = [acc5[c : c + 1] for c in range(6)]
        turn = cross(a, sums[:3])
        pull = cross(x, sums5[:3])
        return vel + [turn[c] - (pull[c] - sums5[3 + c]) for c in range(3)]

    pad2 = jnp.zeros((2, 256), F32)
    pad5 = jnp.zeros((5, 256), F32)
    for blk in range(12):
        rows = tr[blk]
        if blk < 8:
            out = jnp.concatenate([*finish(rows, acct[blk], None), pad5], axis=0)
            rt[2 * blk, :, 0:128] = out[:, :128]
            rt[2 * blk + 1, :, 0:128] = out[:, 128:]
        else:
            out = jnp.concatenate([*finish(rows, acct[blk], acct5[blk - 8]), pad2], axis=0)
            for h in range(2):
                one, two = PAIRS[2 * (blk - 8) + h]
                half = out[:, 128 * h : 128 * h + 128]
                rt[one, :, 128:256] = half
                rt[two, :, 128:256] = pltpu.roll(half, 64, 1)
    for n, (one, two) in enumerate(COUPLES):
        for slot, back in ((one, False), (two, True)):
            if slot is None:
                continue
            more = [accp[n], accp5[n]]
            if back:
                more = [pltpu.roll(v, 64, 1) for v in more]
            blob_part = finish(gsb[slot], accs[slot, :, :128], None)
            full = finish(gsp[slot], accs[slot, :, 128:] + more[0], accs5[slot] + more[1])
            rs[slot, :, 0:128] = jnp.concatenate([*blob_part, pad5[:, :128]], axis=0)
            rs[slot, :, 128:256] = jnp.concatenate([*full, pad2[:, :128]], axis=0)

    def t_result(d):
        return pltpu.make_async_remote_copy(rt.at[d], it.at[d - 1], tsend.at[d - 1], trecv.at[d - 1], device_id=on_plane(a + d), device_id_type=MESH)

    def s_result(d):
        return pltpu.make_async_remote_copy(rs.at[d], is_.at[d - 1], ssend.at[d - 1], srecv.at[d - 1], device_id=on_line(b + d), device_id_type=MESH)

    @pl.loop(1, RING)
    def _(d):
        t_result(d).start()

    @pl.loop(1, NS)
    def _(d):
        s_result(d).start()

    @pl.loop(1, RING)
    def _(d):
        t_result(d).wait()

    @pl.loop(1, NS)
    def _(d):
        s_result(d).wait()

    leave.wait()
    total = rt[0] + rs[0]
    for n in range(RING - 1):
        total = total + it[n]
    for n in range(NS - 1):
        total = total + is_[n]
    total = total * -kernel_scale
    slots = rates.shape[1]
    lane = lax.broadcasted_iota(jnp.int32, (6, slots), 1)
    rates[...] = jnp.where(lane < live[0], total[0:6, 128 : 128 + slots], 0.0)
    blob[...] = total[0:3, 0:128]


def emit_kernel(grid, rates, blob, grid_out, rates_out, blob_out, held, rates_held, blob_held, come, go):
    ways = [(grid.at[c], held.at[c], grid_out.at[c]) for c in range(3)]
    ways += [(rates, rates_held, rates_out), (blob, blob_held, blob_out)]
    copies = [(pltpu.make_async_copy(a, b, come.at[n]), pltpu.make_async_copy(b, c, go.at[n])) for n, (a, b, c) in enumerate(ways)]
    for first, _ in copies:
        first.start()
    for first, second in copies:
        first.wait()
        second.start()
    for _, second in copies:
        second.wait()


def emit(*arrays):
    anywhere = pl.BlockSpec(memory_space=pl.ANY)
    return pl.pallas_call(
        emit_kernel,
        out_shape=tuple(jax.ShapeDtypeStruct(v.shape, v.dtype) for v in arrays),
        in_specs=[anywhere] * len(arrays),
        out_specs=(anywhere,) * len(arrays),
        scratch_shapes=[*[pltpu.VMEM(v.shape, v.dtype) for v in arrays], pltpu.SemaphoreType.DMA((5,)), pltpu.SemaphoreType.DMA((5,))],
        compiler_params=pltpu.CompilerParams(vmem_limit_bytes=60 * 1024 * 1024),
        name="emit",
    )(*arrays)


def per_device(positions, strengths, live_counts, vorticity, diffusivity, seed_counts):
    nx, ny, nz = diffusivity.shape
    vmem = pl.BlockSpec(memory_space=pltpu.VMEM)
    anywhere = pl.BlockSpec(memory_space=pl.ANY)
    dma = pltpu.SemaphoreType.DMA
    results = pl.pallas_call(
        step_kernel,
        out_shape=(
            jax.ShapeDtypeStruct(vorticity.shape, F32),
            jax.ShapeDtypeStruct((6, 64), F32),
            jax.ShapeDtypeStruct((3, 128), F32),
        ),
        in_specs=[anywhere] * 5 + [pl.BlockSpec(memory_space=pltpu.SMEM)],
        out_specs=(anywhere, vmem, vmem),
        scratch_shapes=[
            pltpu.VMEM(vorticity.shape, F32),
            pltpu.VMEM(diffusivity.shape, F32),
            pltpu.VMEM(seed_counts.shape, jnp.int32),
            pltpu.VMEM(positions.shape, F32),
            pltpu.VMEM(strengths.shape, F32),
            dma((5,)),
            pltpu.VMEM((2, 3, ny, nz), F32),
            pltpu.VMEM((2, 48, nz), F32),
            pltpu.VMEM((2, 48, nz), F32),
            pltpu.VMEM((8, 128), F32),
            pltpu.VMEM((8, 128), F32),
            pltpu.VMEM((16, 8, 128), F32),
            pltpu.VMEM((16, 8, 128), F32),
            pltpu.VMEM((NS, 8, 128), F32),
            pltpu.VMEM((NS, 8, 128), F32),
            pltpu.VMEM((3, ny, nz), F32),
            pltpu.VMEM((2, ny, nz), F32),
            dma((4,)),
            dma((4,)),
            dma((15,)),
            dma((15,)),
            dma((8,)),
            dma((8,)),
            dma((15,)),
            dma((15,)),
            dma((8,)),
            dma((8,)),
            pltpu.VMEM(vorticity.shape, F32),
            dma,
            pltpu.VMEM((16, 8, 256), F32),
            pltpu.VMEM((NS, 8, 256), F32),
            pltpu.VMEM((12, 8, 256), F32),
            pltpu.VMEM((24, 32, 256), BF16),
            pltpu.VMEM((NS, 32, 256), BF16),
            pltpu.VMEM((3, NS, 192, 128), F32),
            pltpu.VMEM((3, NS, 64, 128), F32),
            pltpu.VMEM((12, 8, 256), F32),
            pltpu.VMEM((4, 8, 256), F32),
            pltpu.VMEM((NS, 8, 256), F32),
            pltpu.VMEM((NS, 8, 128), F32),
            pltpu.VMEM((5, 32, 128), BF16),
            pltpu.VMEM((3, 5, 128, 128), F32),
            pltpu.VMEM((3, 5, 128, 128), F32),
            pltpu.VMEM((5, 8, 128), F32),
            pltpu.VMEM((5, 8, 128), F32),
            pltpu.VMEM((24, 1, 256), F32),
            *([pltpu.VMEM((192, 512), BF16)] * 2 + [pltpu.VMEM((128, 512), BF16)] * 4) * 2,
            pltpu.VMEM((15, 8, 256), F32),
            pltpu.VMEM((NS - 1, 8, 256), F32),
            dma((15,)),
            dma((15,)),
            dma((NS - 1,)),
            dma((NS - 1,)),
        ],
        compiler_params=pltpu.CompilerParams(vmem_limit_bytes=60 * 1024 * 1024, collective_id=0, has_side_effects=True),
        name="step",
    )(vorticity, diffusivity, seed_counts, positions, strengths, live_counts)
    return emit(*results)


def solution(mesh):
    placed = (
        P(None, ("tgt", "src", "grp")),
        P(None, ("tgt", "src", "grp")),
        P(("tgt", "src", "grp")),
        P(None, "tgt", ("src", "grp"), None),
        P("tgt", ("src", "grp"), None),
        P("tgt", ("src", "grp"), None),
    )
    return jax.shard_map(
        per_device,
        mesh=mesh,
        in_specs=placed,
        out_specs=(
            P(None, "tgt", ("src", "grp"), None),
            P(None, ("tgt", "src", "grp")),
            P(None, ("tgt", "src", "grp")),
        ),
        check_vma=False,
    )
```

```python
import jax
import jax.numpy as jnp
from jax import lax
from jax.experimental import pallas as pl
from jax.experimental.pallas import tpu as pltpu
from jax.sharding import PartitionSpec as P

kernel_scale = 0.25 / 3.141592653589793
seed_weight = 0.0001

SIGMA = 0.0004
F32, BF16 = jnp.float32, jnp.bfloat16
PAIRS = ((0, 8), (1, 2), (3, 4), (5, 6), (7, 9), (10, 11), (12, 13), (14, 15))
NS = 9
COUPLES = ((1, 2), (3, 4), (5, 6), (7, None), (0, 8))


def cross(a, b):
    return (
        a[1] * b[2] - a[2] * b[1],
        a[2] * b[0] - a[0] * b[2],
        a[0] * b[1] - a[1] * b[0],
    )


def pieces(rows):
    one = rows.astype(BF16)
    rest = rows - one.astype(F32)
    two = rest.astype(BF16)
    three = (rest - two.astype(F32)).astype(BF16)
    return one, two, three


def weights_of(rows):
    x = [rows[c : c + 1] for c in range(3)]
    a = [rows[c + 3 : c + 4] for c in range(3)]
    b = cross(x, a)
    zero = jnp.zeros_like(a[0])
    return jnp.concatenate([*a, *b, zero, zero], axis=0)


def stacked(rows):
    one, two, three = pieces(rows)
    return jnp.concatenate([one, two, three, jnp.zeros_like(one)], axis=0)


def fold3(m):
    return m[0:8] + m[8:16] + m[16:24]


def fold2(m):
    return m[0:8] + m[8:16]


NN = (((1,), (0,)), ((), ()))
NT = (((1,), (1,)), ((), ()))


def mm(a, b, dims):
    return lax.dot_general(a, b, dims, preferred_element_type=F32)


MESH = pl.DeviceIdType.MESH
RING = 16


def place():
    tgt, src = lax.axis_index("tgt"), lax.axis_index("src")
    return src * 2 + tgt // 8, lax.rem(tgt, 8) * 2 + lax.axis_index("grp")


def on_plane(a):
    a = lax.rem(a, RING)
    return {"tgt": lax.rem(a, 2) * 8 + lax.rem(lax.axis_index("tgt"), 8), "src": a // 2}


def on_line(b):
    b = lax.rem(b, RING)
    return {"tgt": (lax.axis_index("tgt") // 8) * 8 + b // 2, "grp": lax.rem(b, 2)}


def on_tgt(u):
    return {"tgt": lax.rem(u, RING)}


def on_side(p):
    p = lax.rem(p, RING)
    return {"src": p // 2, "grp": lax.rem(p, 2)}


def step_kernel(vort_in, diff_in, seeds_in, pos_in, stren_in, live, vnext, rates, blob, vort, diff, seeds, pos, stren, local, hx, hy, sy, elp, elb, gtb, gtp, gsb, gsp, gaccs, accw, halo_send, halo_recv, tps, tpr, sps, spr, tbs, tbr, sbs, sbr, vnew, out_sem, rt, rs, tr, wt, ws, scol, acol, acct, acct5, accs, accs5, wp, pcol, pacol, accp, accp5, tmask, khi0, klo0, qhi0, qlo0, uhi0, ulo0, khi1, klo1, qhi1, qlo1, uhi1, ulo1, it, is_, tsend, trecv, ssend, srecv):
    u, p = lax.axis_index("tgt"), lax.axis_index("src") * 2 + lax.axis_index("grp")
    a, b = place()
    fetch = [pltpu.make_async_copy(src, dst, local.at[n]) for n, (src, dst) in enumerate(((pos_in, pos), (stren_in, stren), (vort_in, vort), (diff_in, diff), (seeds_in, seeds)))]
    for copy in fetch:
        copy.start()
    barrier = pltpu.get_barrier_semaphore()
    for to in (on_tgt(u + 1), on_tgt(u + RING - 1), on_side(p + 1), on_side(p + RING - 1)):
        pl.semaphore_signal(barrier, inc=1, device_id=to, device_id_type=MESH)

    @pl.loop(1, RING)
    def _(d):
        pl.semaphore_signal(barrier, inc=1, device_id=on_plane(a + d), device_id_type=MESH)
        pl.semaphore_signal(barrier, inc=1, device_id=on_line(b + d), device_id_type=MESH)

    nx, ny, nz = diff.shape
    fetch[0].wait()
    fetch[1].wait()
    fetch[2].wait()
    for c in range(3):
        sy[0, 16 * c : 16 * c + nx, :] = vort[c, :, 0, :]
        sy[1, 16 * c : 16 * c + nx, :] = vort[c, :, ny - 1, :]
    slots = pos.shape[1]
    elp[...] = jnp.zeros_like(elp)
    elp[0:3, 0:slots] = pos[...]
    lane = lax.broadcasted_iota(jnp.int32, (3, slots), 1)
    elp[3:6, 0:slots] = jnp.where(lane < live[0], stren[...], 0.0)
    pl.semaphore_wait(barrier, 2 * (RING - 1) + 4)

    halos = []
    for n, (src, dst, to) in enumerate(
        (
            (vort.at[:, 0], hx.at[1], on_tgt(u + RING - 1)),
            (vort.at[:, nx - 1], hx.at[0], on_tgt(u + 1)),
            (sy.at[0], hy.at[1], on_side(p + RING - 1)),
            (sy.at[1], hy.at[0], on_side(p + 1)),
        )
    ):
        halos.append(pltpu.make_async_remote_copy(src, dst, halo_send.at[n], halo_recv.at[n], device_id=to, device_id_type=MESH))
    for copy in halos:
        copy.start()

    def tgt_copy(src, held, send, recv, d):
        return pltpu.make_async_remote_copy(src, held.at[RING - d], send, recv, device_id=on_plane(a + d), device_id_type=MESH)

    def tgt_all(held, send, recv):
        every = held.at[pl.ds(1, RING - 1)]
        return pltpu.make_async_remote_copy(every, every, send, recv, device_id=on_plane(a + 1), device_id_type=MESH)

    def side_all(held, send, recv):
        every = held.at[pl.ds(1, NS - 1)]
        return pltpu.make_async_remote_copy(every, every, send, recv, device_id=on_line(b + 1), device_id_type=MESH)

    def side_copy(src, held, send, recv, d):
        return pltpu.make_async_remote_copy(src, held.at[d], send, recv, device_id=on_line(b + RING - d), device_id_type=MESH)

    @pl.loop(1, RING)
    def _(d):
        tgt_copy(elp, gtp, tps, tpr, d).start()

    @pl.loop(1, NS)
    def _(d):
        side_copy(elp, gsp, sps, spr, d).start()

    fetch[3].wait()
    fetch[4].wait()
    row = lax.broadcasted_iota(jnp.int32, (ny, nz), 0)
    col = lax.broadcasted_iota(jnp.int32, (ny, nz), 1)
    gaccs[...] = jnp.zeros_like(gaccs)
    accw[...] = jnp.zeros_like(accw)

    def plane(i, low, high):
        counts = seeds[i].astype(F32)
        weight = counts + 1.0
        accw[0] += weight
        accw[1] += weight * jnp.asarray(i, jnp.int32).astype(F32)
        rate = diff[i]
        for c in range(3):
            v = vort[c, i]
            beside = jnp.where(row > 0, pltpu.roll(v, 1, 0), 0.0)
            beside += jnp.where(row < ny - 1, pltpu.roll(v, ny - 1, 0), 0.0)
            beside += jnp.where(col > 0, pltpu.roll(v, 1, 1), 0.0)
            beside += jnp.where(col < nz - 1, pltpu.roll(v, nz - 1, 1), 0.0)
            if low:
                beside += vort[c, i - 1]
            if high:
                beside += vort[c, i + 1]
            new = v + rate * (beside - 6.0 * v)
            vnew[c, i] = new
            gaccs[c] += counts * new

    plane(0, False, True)

    @pl.loop(1, nx - 1)
    def _(i):
        plane(i, True, True)

    plane(nx - 1, True, False)

    for copy in halos:
        copy.wait()
    sides = [
        [(u > 0).astype(F32), (u < RING - 1).astype(F32)],
        [(p > 0).astype(F32), (p < RING - 1).astype(F32)],
    ]
    extra = []
    for end, i in enumerate((0, nx - 1)):
        counts = seeds[i].astype(F32)
        rate = diff[i] * sides[0][end]
        for c in range(3):
            more = rate * hx[end, c]
            vnew[c, i] += more
            gaccs[c] += counts * more
    edge = [jnp.zeros((1, nz), F32) for _ in range(3)]
    for end, j in enumerate((0, ny - 1)):
        counts = seeds[:, j, :].astype(F32)
        rate = diff[:, j, :] * sides[1][end]
        for c in range(3):
            more = rate * hy[end, 16 * c : 16 * c + nx, :]
            vnew[c, :, j, :] = vnew[c, :, j, :] + more
            edge[c] = edge[c] + jnp.sum(counts * more, axis=0, keepdims=True)

    leave = pltpu.make_async_copy(vnew, vnext, out_sem)
    leave.start()
    weight = accw[0]
    odd = jnp.where(lax.rem(col, 2) == 1, weight, 0.0)
    sums = [jnp.sum(gaccs[c], axis=0, keepdims=True) + edge[c] for c in range(3)]
    sums += [jnp.sum(m, axis=0, keepdims=True) for m in (weight, accw[1], weight * row.astype(F32), odd)]
    sums.append(jnp.zeros((1, nz), F32))
    half = (lax.broadcasted_iota(jnp.int32, (nz, nz // 2), 0) // 2 == lax.broadcasted_iota(jnp.int32, (nz, nz // 2), 1)).astype(F32)
    folded = jnp.dot(jnp.concatenate(sums, axis=0), half, precision=lax.Precision.HIGHEST, preferred_element_type=F32)
    total = folded[3:4]
    block = lax.broadcasted_iota(jnp.int32, (1, nz // 2), 1).astype(F32)
    x = ((u * nx).astype(F32) + 0.5 + folded[4:5] / total) / nz
    y = ((p * ny).astype(F32) + 0.5 + folded[5:6] / total) / nz
    z = (2.0 * block + 0.5 + folded[6:7] / total) / nz
    zero = jnp.zeros_like(x)
    elb[...] = jnp.concatenate([x, y, z, *[folded[c : c + 1] * seed_weight for c in range(3)], zero, zero], axis=0)

    @pl.loop(1, RING)
    def _(d):
        tgt_copy(elb, gtb, tbs, tbr, d).start()

    @pl.loop(1, NS)
    def _(d):
        side_copy(elb, gsb, sbs, sbr, d).start()

    gtb[0] = elb[...]
    gsb[0] = elb[...]
    gtp[0] = elp[...]
    gsp[0] = elp[...]

    tgt_all(gtp, tps, tpr).wait()

    side_all(gsp, sps, spr).wait()

    lane = lax.broadcasted_iota(jnp.int32, (8, 128), 1)
    lane2 = lax.broadcasted_iota(jnp.int32, (1, 256), 1)
    def target_block(blk):
        if blk < 8:
            halves = [gtb[2 * blk], gtb[2 * blk + 1]]
            slots = [2 * blk, 2 * blk, 2 * blk + 1, 2 * blk + 1]
        else:
            slots = [s for h in range(2) for s in PAIRS[2 * (blk - 8) + h]]
            halves = [jnp.where(lane < 64, gtp[one], pltpu.roll(gtp[two], 64, 1)) for one, two in (slots[:2], slots[2:])]
        rows = jnp.concatenate(halves, axis=1)
        tr[blk] = rows
        w = weights_of(rows)
        wt[blk] = stacked(w)
        tmask[blk] = jnp.ones((1, 256), F32)
        both = jnp.zeros((1, 256), F32)
        here = jnp.zeros((1, 256), F32)
        for n, slot in enumerate(slots):
            quarter = (lane2 >= 64 * n) & (lane2 < 64 * n + 64)
            if 1 <= slot <= 7:
                both = jnp.where(quarter, 1.0, both)
            if slot <= 8:
                here = jnp.where(quarter, 1.0, here)
        wt[blk + 12] = stacked(w * both)
        tmask[blk + 12] = here

    for blk in range(8, 12):
        target_block(blk)
    for n, (one, two) in enumerate(COUPLES):
        second = 0.0 if two is None else pltpu.roll(gsp[two], 64, 1)
        couple = jnp.where(lane < 64, gsp[one], second)
        wp[n] = stacked(weights_of(couple))
        across = couple.T
        for c in range(3):
            spread = jnp.broadcast_to(across[:, c : c + 1], (128, 128))
            turn = jnp.broadcast_to(across[:, c + 3 : c + 4] * -3.0, (128, 128))
            pcol[c, n] = spread
            pacol[c, n] = turn
            scol[c, one, 128:192, :] = spread[:64]
            acol[c, one] = turn[:64]
            if two is not None:
                scol[c, two, 128:192, :] = spread[64:]
                acol[c, two] = turn[64:]
    for ref in (acct, acct5, accs, accs5, accp, accp5):
        ref[...] = jnp.zeros_like(ref)

    def split(x, high, low, rows, cols):
        hi = x.astype(BF16)
        high[rows, cols] = hi
        low[rows, cols] = (x - hi.astype(F32)).astype(BF16)

    WIDE = 4

    def values(kind, slot, blk, held):
        khi, klo, qhi, qlo, uhi, ulo = held

        def row(c, h):
            return tr[blk + h // 2, c : c + 1, 128 * (h % 2) : 128 * (h % 2) + 128]

        for pair in range(WIDE // 2):
            lanes = range(2 * pair, 2 * pair + 2)
            tx = {h: [jnp.broadcast_to(row(c, h), (16, 128)) for c in range(3)] for h in lanes}
            if kind != "b":
                ta = {h: [jnp.broadcast_to(row(c + 3, h) * 3.0, (16, 128)) for c in range(3)] for h in lanes}
            for g in range(12 if kind == "b" else 8):
                rows = slice(16 * g, 16 * g + 16)
                turned = kind == "p" or g >= 8
                if kind == "p":
                    sx = [pcol[c, slot, rows, :] for c in range(3)]
                    sa = [pacol[c, slot, rows, :] for c in range(3)]
                    part_rows = rows
                else:
                    sx = [scol[c, slot, rows, :] for c in range(3)]
                    if turned:
                        part_rows = slice(16 * (g - 8), 16 * (g - 8) + 16)
                        sa = [acol[c, slot, part_rows, :] for c in range(3)]
                for h in lanes:
                    cols = slice(128 * h, 128 * h + 128)
                    d = [tx[h][c] - sx[c] for c in range(3)]
                    q = (d[0] * d[0] + d[1] * d[1]) + (d[2] * d[2] + SIGMA)
                    inv = lax.rsqrt(q)
                    inv2 = inv * inv
                    k = inv2 * inv
                    split(k, khi, klo, rows, cols)
                    if kind != "b" or turned:
                        k5 = k * inv2
                    if kind != "b":
                        split(k5 * ((ta[h][0] * d[0] + ta[h][1] * d[1]) + ta[h][2] * d[2]), qhi, qlo, rows, cols)
                    if turned:
                        split(k5 * ((sa[0] * d[0] + sa[1] * d[1]) + sa[2] * d[2]), uhi, ulo, part_rows, cols)

    def sums(kind, slot, blk, side, held):
        khi, klo, qhi, qlo, uhi, ulo = held
        which = [blk + 12 * side + n for n in range(WIDE // 2)]
        v = jnp.concatenate([wt[n] for n in which], axis=1)
        if kind == "b":
            w = ws[slot][:, :192]
        elif kind == "m":
            w = ws[slot][:, :128]
        else:
            w = wp[slot]
        n = w.shape[1]

        def down(high, low):
            return fold3(mm(w, high[:n], NN)) + fold2(mm(w[:16], low[:n], NN))

        def over(high, low, m):
            return fold3(mm(v, high[:m], NT)) + fold2(mm(v[:16], low[:m], NT))

        first = down(khi, klo)
        for j, m in enumerate(which):
            acct[blk + j] += first[:, 256 * j : 256 * j + 256] * tmask[m]
        if kind != "b":
            first = down(qhi, qlo)
            for j, m in enumerate(which):
                acct5[blk + j - 8] += first[:, 256 * j : 256 * j + 256] * tmask[m]
        if kind == "p":
            accp[slot] += over(khi, klo, 128)
            accp5[slot] += over(uhi, ulo, 128)
        else:
            accs[slot, :, :n] += over(khi, klo, n)
        if kind == "b":
            accs5[slot, :, :64] += over(uhi, ulo, 64)

    held0 = (khi0, klo0, qhi0, qlo0, uhi0, ulo0)
    held1 = (khi1, klo1, qhi1, qlo1, uhi1, ulo1)
    def run(kind, first, per, main, extra, place_of):
        for ref in held1:
            ref[...] = jnp.zeros_like(ref)
        zero = jnp.int32(0)

        def step(m, last):
            one, two = place_of(m, m < main, first, per, main)
            values(kind, one[0], one[1], held0)
            sums(kind, *last, held1)
            values(kind, two[0], two[1], held1)
            sums(kind, *one, held0)
            return two

        last = lax.fori_loop(0, main + extra, step, (zero, zero + first, zero), unroll=3)
        sums(kind, *last, held1)

    def blob_place(m, inner, first, per, main):
        slot = jnp.where(inner, 1 + m // per, 0)
        blk = jnp.where(inner, 4 * lax.rem(m, per), 2 * (m - main))
        side = jnp.where(inner, 0, 1)
        return (slot, blk, side), (jnp.where(inner, slot, 8), jnp.where(inner, blk + 2, blk), side)

    def mixed_place(m, inner, first, per, main):
        slot = jnp.where(inner, m + 1, 8 * (m - main))
        side = jnp.where(inner, 0, 1)
        return (slot, jnp.int32(8), side), (slot, jnp.int32(10), side)

    def couple_place(m, inner, first, per, main):
        side = jnp.where(inner, 0, 1)
        return (m, jnp.int32(8), side), (m, jnp.int32(10), side)

    run("p", 8, 1, 4, 1, couple_place)
    tgt_all(gtb, tbs, tbr).wait()

    side_all(gsb, sbs, sbr).wait()

    for blk in range(8):
        target_block(blk)
    for slot in range(NS):
        ws[slot] = stacked(weights_of(jnp.concatenate([gsb[slot], gsp[slot]], axis=1)))
        across = gsb[slot].T
        for c in range(3):
            scol[c, slot, 0:128, :] = jnp.broadcast_to(across[:, c : c + 1], (128, 128))
    run("b", 0, 2, 14, 3, blob_place)
    run("m", 8, 1, 7, 2, mixed_place)

    def finish(rows, acc, acc5):
        x = [rows[c : c + 1] for c in range(3)]
        a = [rows[c + 3 : c + 4] for c in range(3)]
        sums = [acc[c : c + 1] for c in range(6)]
        vel = [m - n for m, n in zip(cross(x, sums[:3]), sums[3:])]
        if acc5 is None:
            return vel
        sums5 = [acc5[c : c + 1] for c in range(6)]
        turn = cross(a, sums[:3])
        pull = cross(x, sums5[:3])
        return vel + [turn[c] - (pull[c] - sums5[3 + c]) for c in range(3)]

    pad2 = jnp.zeros((2, 256), F32)
    pad5 = jnp.zeros((5, 256), F32)
    for blk in range(12):
        rows = tr[blk]
        if blk < 8:
            out = jnp.concatenate([*finish(rows, acct[blk], None), pad5], axis=0)
            rt[2 * blk, :, 0:128] = out[:, :128]
            rt[2 * blk + 1, :, 0:128] = out[:, 128:]
        else:
            out = jnp.concatenate([*finish(rows, acct[blk], acct5[blk - 8]), pad2], axis=0)
            for h in range(2):
                one, two = PAIRS[2 * (blk - 8) + h]
                half = out[:, 128 * h : 128 * h + 128]
                rt[one, :, 128:256] = half
                rt[two, :, 128:256] = pltpu.roll(half, 64, 1)
    for n, (one, two) in enumerate(COUPLES):
        for slot, back in ((one, False), (two, True)):
            if slot is None:
                continue
            more = [accp[n], accp5[n]]
            if back:
                more = [pltpu.roll(v, 64, 1) for v in more]
            blob_part = finish(gsb[slot], accs[slot, :, :128], None)
            full = finish(gsp[slot], accs[slot, :, 128:] + more[0], accs5[slot] + more[1])
            rs[slot, :, 0:128] = jnp.concatenate([*blob_part, pad5[:, :128]], axis=0)
            rs[slot, :, 128:256] = jnp.concatenate([*full, pad2[:, :128]], axis=0)

    def t_result(d):
        return pltpu.make_async_remote_copy(rt.at[d], it.at[d - 1], tsend, trecv, device_id=on_plane(a + d), device_id_type=MESH)

    def s_result(d):
        return pltpu.make_async_remote_copy(rs.at[d], is_.at[d - 1], ssend, srecv, device_id=on_line(b + d), device_id_type=MESH)

    @pl.loop(1, RING)
    def _(d):
        t_result(d).start()

    @pl.loop(1, NS)
    def _(d):
        s_result(d).start()

    pltpu.make_async_remote_copy(it, it, tsend, trecv, device_id=on_plane(a + 1), device_id_type=MESH).wait()

    pltpu.make_async_remote_copy(is_, is_, ssend, srecv, device_id=on_line(b + 1), device_id_type=MESH).wait()

    leave.wait()
    total = rt[0] + rs[0]
    for n in range(RING - 1):
        total = total + it[n]
    for n in range(NS - 1):
        total = total + is_[n]
    total = total * -kernel_scale
    slots = rates.shape[1]
    lane = lax.broadcasted_iota(jnp.int32, (6, slots), 1)
    rates[...] = jnp.where(lane < live[0], total[0:6, 128 : 128 + slots], 0.0)
    blob[...] = total[0:3, 0:128]


def emit_kernel(grid, rates, blob, grid_out, rates_out, blob_out, held, rates_held, blob_held, come, go):
    ways = [(grid.at[c], held.at[c], grid_out.at[c]) for c in range(3)]
    ways += [(rates, rates_held, rates_out), (blob, blob_held, blob_out)]
    copies = [(pltpu.make_async_copy(a, b, come.at[n]), pltpu.make_async_copy(b, c, go.at[n])) for n, (a, b, c) in enumerate(ways)]
    for first, _ in copies:
        first.start()
    for first, second in copies:
        first.wait()
        second.start()
    for _, second in copies:
        second.wait()


def emit(*arrays):
    anywhere = pl.BlockSpec(memory_space=pl.ANY)
    return pl.pallas_call(
        emit_kernel,
        out_shape=tuple(jax.ShapeDtypeStruct(v.shape, v.dtype) for v in arrays),
        in_specs=[anywhere] * len(arrays),
        out_specs=(anywhere,) * len(arrays),
        scratch_shapes=[*[pltpu.VMEM(v.shape, v.dtype) for v in arrays], pltpu.SemaphoreType.DMA((5,)), pltpu.SemaphoreType.DMA((5,))],
        compiler_params=pltpu.CompilerParams(vmem_limit_bytes=60 * 1024 * 1024),
        name="emit",
    )(*arrays)


def per_device(positions, strengths, live_counts, vorticity, diffusivity, seed_counts):
    nx, ny, nz = diffusivity.shape
    vmem = pl.BlockSpec(memory_space=pltpu.VMEM)
    anywhere = pl.BlockSpec(memory_space=pl.ANY)
    dma = pltpu.SemaphoreType.DMA
    results = pl.pallas_call(
        step_kernel,
        out_shape=(
            jax.ShapeDtypeStruct(vorticity.shape, F32),
            jax.ShapeDtypeStruct((6, 64), F32),
            jax.ShapeDtypeStruct((3, 128), F32),
        ),
        in_specs=[anywhere] * 5 + [pl.BlockSpec(memory_space=pltpu.SMEM)],
        out_specs=(anywhere, vmem, vmem),
        scratch_shapes=[
            pltpu.VMEM(vorticity.shape, F32),
            pltpu.VMEM(diffusivity.shape, F32),
            pltpu.VMEM(seed_counts.shape, jnp.int32),
            pltpu.VMEM(positions.shape, F32),
            pltpu.VMEM(strengths.shape, F32),
            dma((5,)),
            pltpu.VMEM((2, 3, ny, nz), F32),
            pltpu.VMEM((2, 48, nz), F32),
            pltpu.VMEM((2, 48, nz), F32),
            pltpu.VMEM((8, 128), F32),
            pltpu.VMEM((8, 128), F32),
            pltpu.VMEM((16, 8, 128), F32),
            pltpu.VMEM((16, 8, 128), F32),
            pltpu.VMEM((NS, 8, 128), F32),
            pltpu.VMEM((NS, 8, 128), F32),
            pltpu.VMEM((3, ny, nz), F32),
            pltpu.VMEM((2, ny, nz), F32),
            dma((4,)),
            dma((4,)),
            dma,
            dma,
            dma,
            dma,
            dma,
            dma,
            dma,
            dma,
            pltpu.VMEM(vorticity.shape, F32),
            dma,
            pltpu.VMEM((16, 8, 256), F32),
            pltpu.VMEM((NS, 8, 256), F32),
            pltpu.VMEM((12, 8, 256), F32),
            pltpu.VMEM((24, 32, 256), BF16),
            pltpu.VMEM((NS, 32, 256), BF16),
            pltpu.VMEM((3, NS, 192, 128), F32),
            pltpu.VMEM((3, NS, 64, 128), F32),
            pltpu.VMEM((12, 8, 256), F32),
            pltpu.VMEM((4, 8, 256), F32),
            pltpu.VMEM((NS, 8, 256), F32),
            pltpu.VMEM((NS, 8, 128), F32),
            pltpu.VMEM((5, 32, 128), BF16),
            pltpu.VMEM((3, 5, 128, 128), F32),
            pltpu.VMEM((3, 5, 128, 128), F32),
            pltpu.VMEM((5, 8, 128), F32),
            pltpu.VMEM((5, 8, 128), F32),
            pltpu.VMEM((24, 1, 256), F32),
            *([pltpu.VMEM((192, 512), BF16)] * 2 + [pltpu.VMEM((128, 512), BF16)] * 4) * 2,
            pltpu.VMEM((15, 8, 256), F32),
            pltpu.VMEM((NS - 1, 8, 256), F32),
            dma,
            dma,
            dma,
            dma,
        ],
        compiler_params=pltpu.CompilerParams(vmem_limit_bytes=60 * 1024 * 1024, collective_id=0, has_side_effects=True),
        name="step",
    )(vorticity, diffusivity, seed_counts, positions, strengths, live_counts)
    return emit(*results)


def solution(mesh):
    placed = (
        P(None, ("tgt", "src", "grp")),
        P(None, ("tgt", "src", "grp")),
        P(("tgt", "src", "grp")),
        P(None, "tgt", ("src", "grp"), None),
        P("tgt", ("src", "grp"), None),
        P("tgt", ("src", "grp"), None),
    )
    return jax.shard_map(
        per_device,
        mesh=mesh,
        in_specs=placed,
        out_specs=(
            P(None, "tgt", ("src", "grp"), None),
            P(None, ("tgt", "src", "grp")),
            P(None, ("tgt", "src", "grp")),
        ),
        check_vma=False,
    )
```

```python
import jax
import jax.numpy as jnp
from jax import lax
from jax.experimental import pallas as pl
from jax.experimental.pallas import tpu as pltpu
from jax.sharding import PartitionSpec as P

kernel_scale = 0.25 / 3.141592653589793
seed_weight = 0.0001

SIGMA = 0.0004
F32, BF16 = jnp.float32, jnp.bfloat16
PAIRS = ((0, 8), (1, 2), (3, 4), (5, 6), (7, 9), (10, 11), (12, 13), (14, 15))
NS = 9
COUPLES = ((1, 2), (3, 4), (5, 6), (7, None), (0, 8))


def cross(a, b):
    return (
        a[1] * b[2] - a[2] * b[1],
        a[2] * b[0] - a[0] * b[2],
        a[0] * b[1] - a[1] * b[0],
    )


def pieces(rows):
    one = rows.astype(BF16)
    rest = rows - one.astype(F32)
    two = rest.astype(BF16)
    three = (rest - two.astype(F32)).astype(BF16)
    return one, two, three


def weights_of(rows):
    x = [rows[c : c + 1] for c in range(3)]
    a = [rows[c + 3 : c + 4] for c in range(3)]
    b = cross(x, a)
    zero = jnp.zeros_like(a[0])
    return jnp.concatenate([*a, *b, zero, zero], axis=0)


def stacked(rows):
    one, two, three = pieces(rows)
    return jnp.concatenate([one, two, three, jnp.zeros_like(one)], axis=0)


def fold3(m):
    return m[0:8] + m[8:16] + m[16:24]


def fold2(m):
    return m[0:8] + m[8:16]


NN = (((1,), (0,)), ((), ()))
NT = (((1,), (1,)), ((), ()))


def mm(a, b, dims):
    return lax.dot_general(a, b, dims, preferred_element_type=F32)


MESH = pl.DeviceIdType.MESH
RING = 16


def place():
    tgt, src = lax.axis_index("tgt"), lax.axis_index("src")
    return src * 2 + tgt // 8, lax.rem(tgt, 8) * 2 + lax.axis_index("grp")


def on_plane(a):
    a = lax.rem(a, RING)
    return {"tgt": lax.rem(a, 2) * 8 + lax.rem(lax.axis_index("tgt"), 8), "src": a // 2}


def on_line(b):
    b = lax.rem(b, RING)
    return {"tgt": (lax.axis_index("tgt") // 8) * 8 + b // 2, "grp": lax.rem(b, 2)}


def on_tgt(u):
    return {"tgt": lax.rem(u, RING)}


def on_side(p):
    p = lax.rem(p, RING)
    return {"src": p // 2, "grp": lax.rem(p, 2)}


def step_kernel(vort_in, diff_in, seeds_in, pos_in, stren_in, live, vnext, rates, blob, vort, diff, seeds, pos, stren, local, hx, hy, sy, elp, elb, gtb, gtp, gsb, gsp, gaccs, accw, halo_send, halo_recv, tps, tpr, sps, spr, tbs, tbr, sbs, sbr, vnew, out_sem, rt, rs, tr, wt, ws, scol, acol, acct, acct5, accs, accs5, wp, pcol, pacol, accp, accp5, tmask, khi0, klo0, qhi0, qlo0, uhi0, ulo0, khi1, klo1, qhi1, qlo1, uhi1, ulo1, it, is_, tsend, trecv, ssend, srecv):
    u, p = lax.axis_index("tgt"), lax.axis_index("src") * 2 + lax.axis_index("grp")
    a, b = place()
    fetch = [pltpu.make_async_copy(src, dst, local.at[n]) for n, (src, dst) in enumerate(((pos_in, pos), (stren_in, stren), (vort_in, vort), (diff_in, diff), (seeds_in, seeds)))]
    for copy in fetch:
        copy.start()
    barrier = pltpu.get_barrier_semaphore()
    for to in (on_tgt(u + 1), on_tgt(u + RING - 1), on_side(p + 1), on_side(p + RING - 1)):
        pl.semaphore_signal(barrier, inc=1, device_id=to, device_id_type=MESH)

    @pl.loop(0, RING - 1)
    def _(e):
        d = lax.rem(e + 5, RING - 1) + 1
        pl.semaphore_signal(barrier, inc=1, device_id=on_line(b + d), device_id_type=MESH)
        pl.semaphore_signal(barrier, inc=1, device_id=on_plane(a + d), device_id_type=MESH)

    nx, ny, nz = diff.shape
    fetch[0].wait()
    fetch[1].wait()
    fetch[2].wait()
    for c in range(3):
        sy[0, 16 * c : 16 * c + nx, :] = vort[c, :, 0, :]
        sy[1, 16 * c : 16 * c + nx, :] = vort[c, :, ny - 1, :]
    slots = pos.shape[1]
    elp[...] = jnp.zeros_like(elp)
    elp[0:3, 0:slots] = pos[...]
    lane = lax.broadcasted_iota(jnp.int32, (3, slots), 1)
    elp[3:6, 0:slots] = jnp.where(lane < live[0], stren[...], 0.0)
    pl.semaphore_wait(barrier, 2 * (RING - 1) + 4)

    halos = []
    for n, (src, dst, to) in enumerate(
        (
            (vort.at[:, 0], hx.at[1], on_tgt(u + RING - 1)),
            (vort.at[:, nx - 1], hx.at[0], on_tgt(u + 1)),
            (sy.at[0], hy.at[1], on_side(p + RING - 1)),
            (sy.at[1], hy.at[0], on_side(p + 1)),
        )
    ):
        halos.append(pltpu.make_async_remote_copy(src, dst, halo_send.at[n], halo_recv.at[n], device_id=to, device_id_type=MESH))
    for copy in halos:
        copy.start()

    def tgt_copy(src, held, send, recv, d):
        return pltpu.make_async_remote_copy(src, held.at[RING - d], send, recv, device_id=on_plane(a + d), device_id_type=MESH)

    def tgt_all(held, send, recv):
        every = held.at[pl.ds(1, RING - 1)]
        return pltpu.make_async_remote_copy(every, every, send, recv, device_id=on_plane(a + 1), device_id_type=MESH)

    def side_all(held, send, recv):
        every = held.at[pl.ds(1, NS - 1)]
        return pltpu.make_async_remote_copy(every, every, send, recv, device_id=on_line(b + 1), device_id_type=MESH)

    def side_copy(src, held, send, recv, d):
        return pltpu.make_async_remote_copy(src, held.at[d], send, recv, device_id=on_line(b + RING - d), device_id_type=MESH)

    @pl.loop(1, NS)
    def _(d):
        side_copy(elp, gsp, sps, spr, NS - d).start()

    @pl.loop(0, RING - 1)
    def _(d):
        tgt_copy(elp, gtp, tps, tpr, lax.rem(d + 4, RING - 1) + 1).start()

    fetch[3].wait()
    fetch[4].wait()
    row = lax.broadcasted_iota(jnp.int32, (ny, nz), 0)
    col = lax.broadcasted_iota(jnp.int32, (ny, nz), 1)
    gaccs[...] = jnp.zeros_like(gaccs)
    accw[...] = jnp.zeros_like(accw)

    def plane(i, low, high):
        counts = seeds[i].astype(F32)
        weight = counts + 1.0
        accw[0] += weight
        accw[1] += weight * jnp.asarray(i, jnp.int32).astype(F32)
        rate = diff[i]
        for c in range(3):
            v = vort[c, i]
            beside = jnp.where(row > 0, pltpu.roll(v, 1, 0), 0.0)
            beside += jnp.where(row < ny - 1, pltpu.roll(v, ny - 1, 0), 0.0)
            beside += jnp.where(col > 0, pltpu.roll(v, 1, 1), 0.0)
            beside += jnp.where(col < nz - 1, pltpu.roll(v, nz - 1, 1), 0.0)
            if low:
                beside += vort[c, i - 1]
            if high:
                beside += vort[c, i + 1]
            new = v + rate * (beside - 6.0 * v)
            vnew[c, i] = new
            gaccs[c] += counts * new

    plane(0, False, True)

    @pl.loop(1, nx - 1)
    def _(i):
        plane(i, True, True)

    plane(nx - 1, True, False)

    for ref in (acct, acct5, accs, accs5, accp, accp5):
        ref[...] = jnp.zeros_like(ref)
    for copy in halos:
        copy.wait()
    sides = [
        [(u > 0).astype(F32), (u < RING - 1).astype(F32)],
        [(p > 0).astype(F32), (p < RING - 1).astype(F32)],
    ]
    extra = []
    for end, i in enumerate((0, nx - 1)):
        counts = seeds[i].astype(F32)
        rate = diff[i] * sides[0][end]
        for c in range(3):
            more = rate * hx[end, c]
            vnew[c, i] += more
            gaccs[c] += counts * more
    edge = [jnp.zeros((1, nz), F32) for _ in range(3)]
    for end, j in enumerate((0, ny - 1)):
        counts = seeds[:, j, :].astype(F32)
        rate = diff[:, j, :] * sides[1][end]
        for c in range(3):
            more = rate * hy[end, 16 * c : 16 * c + nx, :]
            vnew[c, :, j, :] = vnew[c, :, j, :] + more
            edge[c] = edge[c] + jnp.sum(counts * more, axis=0, keepdims=True)

    leave = pltpu.make_async_copy(vnew, vnext, out_sem)
    leave.start()
    weight = accw[0]
    odd = jnp.where(lax.rem(col, 2) == 1, weight, 0.0)
    sums = [jnp.sum(gaccs[c], axis=0, keepdims=True) + edge[c] for c in range(3)]
    sums += [jnp.sum(m, axis=0, keepdims=True) for m in (weight, accw[1], weight * row.astype(F32), odd)]
    sums.append(jnp.zeros((1, nz), F32))
    half = (lax.broadcasted_iota(jnp.int32, (nz, nz // 2), 0) // 2 == lax.broadcasted_iota(jnp.int32, (nz, nz // 2), 1)).astype(F32)
    folded = jnp.dot(jnp.concatenate(sums, axis=0), half, precision=lax.Precision.HIGHEST, preferred_element_type=F32)
    total = folded[3:4]
    block = lax.broadcasted_iota(jnp.int32, (1, nz // 2), 1).astype(F32)
    x = ((u * nx).astype(F32) + 0.5 + folded[4:5] / total) / nz
    y = ((p * ny).astype(F32) + 0.5 + folded[5:6] / total) / nz
    z = (2.0 * block + 0.5 + folded[6:7] / total) / nz
    zero = jnp.zeros_like(x)
    elb[...] = jnp.concatenate([x, y, z, *[folded[c : c + 1] * seed_weight for c in range(3)], zero, zero], axis=0)

    @pl.loop(1, NS)
    def _(d):
        side_copy(elb, gsb, sbs, sbr, NS - d).start()

    @pl.loop(0, RING - 1)
    def _(d):
        tgt_copy(elb, gtb, tbs, tbr, lax.rem(d + 4, RING - 1) + 1).start()

    gtb[0] = elb[...]
    gsb[0] = elb[...]
    gtp[0] = elp[...]
    gsp[0] = elp[...]

    tgt_all(gtp, tps, tpr).wait()

    side_all(gsp, sps, spr).wait()

    lane = lax.broadcasted_iota(jnp.int32, (8, 128), 1)
    lane2 = lax.broadcasted_iota(jnp.int32, (1, 256), 1)
    def target_block(blk):
        if blk < 8:
            halves = [gtb[2 * blk], gtb[2 * blk + 1]]
            slots = [2 * blk, 2 * blk, 2 * blk + 1, 2 * blk + 1]
        else:
            slots = [s for h in range(2) for s in PAIRS[2 * (blk - 8) + h]]
            halves = [jnp.where(lane < 64, gtp[one], pltpu.roll(gtp[two], 64, 1)) for one, two in (slots[:2], slots[2:])]
        rows = jnp.concatenate(halves, axis=1)
        tr[blk] = rows
        w = weights_of(rows)
        wt[blk] = stacked(w)
        tmask[blk] = jnp.ones((1, 256), F32)
        both = jnp.zeros((1, 256), F32)
        here = jnp.zeros((1, 256), F32)
        for n, slot in enumerate(slots):
            quarter = (lane2 >= 64 * n) & (lane2 < 64 * n + 64)
            if 1 <= slot <= 7:
                both = jnp.where(quarter, 1.0, both)
            if slot <= 8:
                here = jnp.where(quarter, 1.0, here)
        wt[blk + 12] = stacked(w * both)
        tmask[blk + 12] = here

    for blk in range(8, 12):
        target_block(blk)
    for n, (one, two) in enumerate(COUPLES):
        second = 0.0 if two is None else pltpu.roll(gsp[two], 64, 1)
        couple = jnp.where(lane < 64, gsp[one], second)
        wp[n] = stacked(weights_of(couple))
        across = couple.T
        for c in range(3):
            spread = jnp.broadcast_to(across[:, c : c + 1], (128, 128))
            turn = jnp.broadcast_to(across[:, c + 3 : c + 4] * -3.0, (128, 128))
            pcol[c, n] = spread
            pacol[c, n] = turn
            scol[c, one, 128:192, :] = spread[:64]
            acol[c, one] = turn[:64]
            if two is not None:
                scol[c, two, 128:192, :] = spread[64:]
                acol[c, two] = turn[64:]

    def split(x, high, low, rows, cols):
        hi = x.astype(BF16)
        high[rows, cols] = hi
        low[rows, cols] = (x - hi.astype(F32)).astype(BF16)

    WIDE = 4

    def values(kind, slot, blk, held):
        khi, klo, qhi, qlo, uhi, ulo = held

        def row(c, h):
            return tr[blk + h // 2, c : c + 1, 128 * (h % 2) : 128 * (h % 2) + 128]

        for pair in range(WIDE // 2):
            lanes = range(2 * pair, 2 * pair + 2)
            tx = {h: [jnp.broadcast_to(row(c, h), (16, 128)) for c in range(3)] for h in lanes}
            if kind != "b":
                ta = {h: [jnp.broadcast_to(row(c + 3, h) * 3.0, (16, 128)) for c in range(3)] for h in lanes}
            for g in range(12 if kind == "b" else 8):
                rows = slice(16 * g, 16 * g + 16)
                turned = kind == "p" or g >= 8
                if kind == "p":
                    sx = [pcol[c, slot, rows, :] for c in range(3)]
                    sa = [pacol[c, slot, rows, :] for c in range(3)]
                    part_rows = rows
                else:
                    sx = [scol[c, slot, rows, :] for c in range(3)]
                    if turned:
                        part_rows = slice(16 * (g - 8), 16 * (g - 8) + 16)
                        sa = [acol[c, slot, part_rows, :] for c in range(3)]
                for h in lanes:
                    cols = slice(128 * h, 128 * h + 128)
                    d = [tx[h][c] - sx[c] for c in range(3)]
                    q = (d[0] * d[0] + d[1] * d[1]) + (d[2] * d[2] + SIGMA)
                    inv = lax.rsqrt(q)
                    inv2 = inv * inv
                    k = inv2 * inv
                    split(k, khi, klo, rows, cols)
                    if kind != "b" or turned:
                        k5 = k * inv2
                    if kind != "b":
                        split(k5 * ((ta[h][0] * d[0] + ta[h][1] * d[1]) + ta[h][2] * d[2]), qhi, qlo, rows, cols)
                    if turned:
                        split(k5 * ((sa[0] * d[0] + sa[1] * d[1]) + sa[2] * d[2]), uhi, ulo, part_rows, cols)

    def sums(kind, slot, blk, side, held):
        khi, klo, qhi, qlo, uhi, ulo = held
        which = [blk + 12 * side + n for n in range(WIDE // 2)]
        v = jnp.concatenate([wt[n] for n in which], axis=1)
        if kind == "b":
            w = ws[slot][:, :192]
        elif kind == "m":
            w = ws[slot][:, :128]
        else:
            w = wp[slot]
        n = w.shape[1]

        def down(high, low):
            return fold3(mm(w, high[:n], NN)) + fold2(mm(w[:16], low[:n], NN))

        def over(high, low, m):
            return fold3(mm(v, high[:m], NT)) + fold2(mm(v[:16], low[:m], NT))

        first = down(khi, klo)
        for j, m in enumerate(which):
            acct[blk + j] += first[:, 256 * j : 256 * j + 256] * tmask[m]
        if kind != "b":
            first = down(qhi, qlo)
            for j, m in enumerate(which):
                acct5[blk + j - 8] += first[:, 256 * j : 256 * j + 256] * tmask[m]
        if kind == "p":
            accp[slot] += over(khi, klo, 128)
            accp5[slot] += over(uhi, ulo, 128)
        else:
            accs[slot, :, :n] += over(khi, klo, n)
        if kind == "b":
            accs5[slot, :, :64] += over(uhi, ulo, 64)

    held0 = (khi0, klo0, qhi0, qlo0, uhi0, ulo0)
    held1 = (khi1, klo1, qhi1, qlo1, uhi1, ulo1)
    def run(kind, first, per, main, extra, place_of):
        for ref in held1:
            ref[...] = jnp.zeros_like(ref)
        zero = jnp.int32(0)

        def step(m, last):
            one, two = place_of(m, m < main, first, per, main)
            values(kind, one[0], one[1], held0)
            sums(kind, *last, held1)
            values(kind, two[0], two[1], held1)
            sums(kind, *one, held0)
            return two

        last = lax.fori_loop(0, main + extra, step, (zero, zero + first, zero), unroll=3)
        sums(kind, *last, held1)

    def blob_place(m, inner, first, per, main):
        slot = jnp.where(inner, 1 + m // per, 0)
        blk = jnp.where(inner, 4 * lax.rem(m, per), 2 * (m - main))
        side = jnp.where(inner, 0, 1)
        return (slot, blk, side), (jnp.where(inner, slot, 8), jnp.where(inner, blk + 2, blk), side)

    def mixed_place(m, inner, first, per, main):
        slot = jnp.where(inner, m + 1, 8 * (m - main))
        side = jnp.where(inner, 0, 1)
        return (slot, jnp.int32(8), side), (slot, jnp.int32(10), side)

    def couple_place(m, inner, first, per, main):
        side = jnp.where(inner, 0, 1)
        return (m, jnp.int32(8), side), (m, jnp.int32(10), side)

    run("p", 8, 1, 4, 1, couple_place)
    tgt_all(gtb, tbs, tbr).wait()

    side_all(gsb, sbs, sbr).wait()

    for blk in range(8):
        target_block(blk)
    for slot in range(NS):
        ws[slot] = stacked(weights_of(jnp.concatenate([gsb[slot], gsp[slot]], axis=1)))
        across = gsb[slot].T
        for c in range(3):
            scol[c, slot, 0:128, :] = jnp.broadcast_to(across[:, c : c + 1], (128, 128))
    run("b", 0, 2, 14, 3, blob_place)
    run("m", 8, 1, 7, 2, mixed_place)

    def finish(rows, acc, acc5):
        x = [rows[c : c + 1] for c in range(3)]
        a = [rows[c + 3 : c + 4] for c in range(3)]
        sums = [acc[c : c + 1] for c in range(6)]
        vel = [m - n for m, n in zip(cross(x, sums[:3]), sums[3:])]
        if acc5 is None:
            return vel
        sums5 = [acc5[c : c + 1] for c in range(6)]
        turn = cross(a, sums[:3])
        pull = cross(x, sums5[:3])
        return vel + [turn[c] - (pull[c] - sums5[3 + c]) for c in range(3)]

    pad2 = jnp.zeros((2, 256), F32)
    pad5 = jnp.zeros((5, 256), F32)
    for blk in range(12):
        rows = tr[blk]
        if blk < 8:
            out = jnp.concatenate([*finish(rows, acct[blk], None), pad5], axis=0)
            rt[2 * blk, :, 0:128] = out[:, :128]
            rt[2 * blk + 1, :, 0:128] = out[:, 128:]
        else:
            out = jnp.concatenate([*finish(rows, acct[blk], acct5[blk - 8]), pad2], axis=0)
            for h in range(2):
                one, two = PAIRS[2 * (blk - 8) + h]
                half = out[:, 128 * h : 128 * h + 128]
                rt[one, :, 128:256] = half
                rt[two, :, 128:256] = pltpu.roll(half, 64, 1)
    for n, (one, two) in enumerate(COUPLES):
        for slot, back in ((one, False), (two, True)):
            if slot is None:
                continue
            more = [accp[n], accp5[n]]
            if back:
                more = [pltpu.roll(v, 64, 1) for v in more]
            blob_part = finish(gsb[slot], accs[slot, :, :128], None)
            full = finish(gsp[slot], accs[slot, :, 128:] + more[0], accs5[slot] + more[1])
            rs[slot, :, 0:128] = jnp.concatenate([*blob_part, pad5[:, :128]], axis=0)
            rs[slot, :, 128:256] = jnp.concatenate([*full, pad2[:, :128]], axis=0)

    def t_result(d):
        return pltpu.make_async_remote_copy(rt.at[d], it.at[d - 1], tsend, trecv, device_id=on_plane(a + d), device_id_type=MESH)

    def s_result(d):
        return pltpu.make_async_remote_copy(rs.at[d], is_.at[d - 1], ssend, srecv, device_id=on_line(b + d), device_id_type=MESH)

    @pl.loop(1, NS)
    def _(d):
        s_result(NS - d).start()

    @pl.loop(0, RING - 1)
    def _(d):
        t_result(lax.rem(d + 4, RING - 1) + 1).start()

    pltpu.make_async_remote_copy(it, it, tsend, trecv, device_id=on_plane(a + 1), device_id_type=MESH).wait()

    pltpu.make_async_remote_copy(is_, is_, ssend, srecv, device_id=on_line(b + 1), device_id_type=MESH).wait()

    leave.wait()
    total = rt[0] + rs[0]
    for n in range(RING - 1):
        total = total + it[n]
    for n in range(NS - 1):
        total = total + is_[n]
    total = total * -kernel_scale
    slots = rates.shape[1]
    lane = lax.broadcasted_iota(jnp.int32, (6, slots), 1)
    rates[...] = jnp.where(lane < live[0], total[0:6, 128 : 128 + slots], 0.0)
    blob[...] = total[0:3, 0:128]


def emit_kernel(grid, rates, blob, grid_out, rates_out, blob_out, held, rates_held, blob_held, come, go):
    ways = [(grid.at[c], held.at[c], grid_out.at[c]) for c in range(3)]
    ways += [(rates, rates_held, rates_out), (blob, blob_held, blob_out)]
    copies = [(pltpu.make_async_copy(a, b, come.at[n]), pltpu.make_async_copy(b, c, go.at[n])) for n, (a, b, c) in enumerate(ways)]
    for first, _ in copies:
        first.start()
    for first, second in copies:
        first.wait()
        second.start()
    for _, second in copies:
        second.wait()


def emit(*arrays):
    anywhere = pl.BlockSpec(memory_space=pl.ANY)
    return pl.pallas_call(
        emit_kernel,
        out_shape=tuple(jax.ShapeDtypeStruct(v.shape, v.dtype) for v in arrays),
        in_specs=[anywhere] * len(arrays),
        out_specs=(anywhere,) * len(arrays),
        scratch_shapes=[*[pltpu.VMEM(v.shape, v.dtype) for v in arrays], pltpu.SemaphoreType.DMA((5,)), pltpu.SemaphoreType.DMA((5,))],
        compiler_params=pltpu.CompilerParams(vmem_limit_bytes=60 * 1024 * 1024),
        name="emit",
    )(*arrays)


def per_device(positions, strengths, live_counts, vorticity, diffusivity, seed_counts):
    nx, ny, nz = diffusivity.shape
    vmem = pl.BlockSpec(memory_space=pltpu.VMEM)
    anywhere = pl.BlockSpec(memory_space=pl.ANY)
    dma = pltpu.SemaphoreType.DMA
    results = pl.pallas_call(
        step_kernel,
        out_shape=(
            jax.ShapeDtypeStruct(vorticity.shape, F32),
            jax.ShapeDtypeStruct((6, 64), F32),
            jax.ShapeDtypeStruct((3, 128), F32),
        ),
        in_specs=[anywhere] * 5 + [pl.BlockSpec(memory_space=pltpu.SMEM)],
        out_specs=(anywhere, vmem, vmem),
        scratch_shapes=[
            pltpu.VMEM(vorticity.shape, F32),
            pltpu.VMEM(diffusivity.shape, F32),
            pltpu.VMEM(seed_counts.shape, jnp.int32),
            pltpu.VMEM(positions.shape, F32),
            pltpu.VMEM(strengths.shape, F32),
            dma((5,)),
            pltpu.VMEM((2, 3, ny, nz), F32),
            pltpu.VMEM((2, 48, nz), F32),
            pltpu.VMEM((2, 48, nz), F32),
            pltpu.VMEM((8, 128), F32),
            pltpu.VMEM((8, 128), F32),
            pltpu.VMEM((16, 8, 128), F32),
            pltpu.VMEM((16, 8, 128), F32),
            pltpu.VMEM((NS, 8, 128), F32),
            pltpu.VMEM((NS, 8, 128), F32),
            pltpu.VMEM((3, ny, nz), F32),
            pltpu.VMEM((2, ny, nz), F32),
            dma((4,)),
            dma((4,)),
            dma,
            dma,
            dma,
            dma,
            dma,
            dma,
            dma,
            dma,
            pltpu.VMEM(vorticity.shape, F32),
            dma,
            pltpu.VMEM((16, 8, 256), F32),
            pltpu.VMEM((NS, 8, 256), F32),
            pltpu.VMEM((12, 8, 256), F32),
            pltpu.VMEM((24, 32, 256), BF16),
            pltpu.VMEM((NS, 32, 256), BF16),
            pltpu.VMEM((3, NS, 192, 128), F32),
            pltpu.VMEM((3, NS, 64, 128), F32),
            pltpu.VMEM((12, 8, 256), F32),
            pltpu.VMEM((4, 8, 256), F32),
            pltpu.VMEM((NS, 8, 256), F32),
            pltpu.VMEM((NS, 8, 128), F32),
            pltpu.VMEM((5, 32, 128), BF16),
            pltpu.VMEM((3, 5, 128, 128), F32),
            pltpu.VMEM((3, 5, 128, 128), F32),
            pltpu.VMEM((5, 8, 128), F32),
            pltpu.VMEM((5, 8, 128), F32),
            pltpu.VMEM((24, 1, 256), F32),
            *([pltpu.VMEM((192, 512), BF16)] * 2 + [pltpu.VMEM((128, 512), BF16)] * 4) * 2,
            pltpu.VMEM((15, 8, 256), F32),
            pltpu.VMEM((NS - 1, 8, 256), F32),
            dma,
            dma,
            dma,
            dma,
        ],
        compiler_params=pltpu.CompilerParams(vmem_limit_bytes=60 * 1024 * 1024, collective_id=0, has_side_effects=True),
        name="step",
    )(vorticity, diffusivity, seed_counts, positions, strengths, live_counts)
    return emit(*results)


def solution(mesh):
    placed = (
        P(None, ("tgt", "src", "grp")),
        P(None, ("tgt", "src", "grp")),
        P(("tgt", "src", "grp")),
        P(None, "tgt", ("src", "grp"), None),
        P("tgt", ("src", "grp"), None),
        P("tgt", ("src", "grp"), None),
    )
    return jax.shard_map(
        per_device,
        mesh=mesh,
        in_specs=placed,
        out_specs=(
            P(None, "tgt", ("src", "grp"), None),
            P(None, ("tgt", "src", "grp")),
            P(None, ("tgt", "src", "grp")),
        ),
        check_vma=False,
    )
```
